32 devices in a mesh: sec: 4 (over y, x), wide: 8 (over z, core).
Axes of the slice: x: 2, y: 2, z: 4, core: 2. Of those that a mesh axis runs over, the one named last changes fastest.
Arguments:
- train_feats: bfloat16 [512, 512], P('wide'), may hold values from -0.26367188 to 0.26367188
- train_targets: float32 [512, 1000], P('wide'), may hold values from -6 to 6
- batch_idx: int32 [32], P('wide'), may hold values from 0 to 511, as said below
- centers: bfloat16 [65536, 512], P(('sec', 'wide')), may hold values from -0.26367188 to 0.26367188
- weights: bfloat16 [65536, 1000], P(('sec', 'wide')), may hold values from -0.0234375 to 0.0234375
- nys_idx: int32 [2048], P('wide'), may hold values from 0 to 65535, as said below
- eig_vecs: float32 [2048, 128], P('wide'), may hold values from -0.25 to 0.25
- eig_scale: float32 [128], replicated, may hold values from 0.2 to 1
Outputs:
- new_weights: bfloat16 [65536, 1000], P(('sec', 'wide'))
- residual: float32 [32, 1000], P('wide')
The draws below stay inside these ranges and needn't reach their ends.
Inputs may be any that keep to these rules, and one draw needn't show every extreme that they name: `batch_idx`: entries k * 4 to (k + 1) * 4 - 1 name training rows k * 64 to (k + 1) * 64 - 1. For entry i, (nys_idx[i] // 2048) modulo (8) equals i // 256; the section, nys_idx[i] // 16384, is any; indices may repeat.
All inputs are finite; a program needn't handle non-finite values.
Results may differ from the reference program's by a relative error of at most 0.0054.
Values may be sent and summed in bfloat16 or wider, within the bound.
No kernel may reach another device: no remote copies, remote signals or barrier semaphores. Data moves between devices by JAX's collectives and lax.ppermute only.
A program may use at most 128 MiB of HBM per device.

```python
import math
import jax
import jax.numpy as jnp
from jax import lax

D = 512
C = 1000
NYS = 2048
K_EIG = 128
C_DEV = 2048
BROWS = 4
POOL_DEV = 64
BATCH = 32
POOL = 512
CENTERS = 65536


def draw_batch_idx(key, part):
    owner = jnp.arange(BATCH, dtype=jnp.int32) // BROWS
    offset = jax.random.randint(key, (BATCH,), 0, POOL_DEV, dtype=jnp.int32)
    return owner * POOL_DEV + offset


def draw_nys_idx(key, part):
    groups = BATCH // BROWS
    sections = CENTERS // (C_DEV * groups)
    owner = jnp.arange(NYS, dtype=jnp.int32) // (NYS // groups)
    key_sec = jax.random.fold_in(key, 11)
    key_off = jax.random.fold_in(key, 12)
    section = jax.random.randint(key_sec, (NYS,), 0, sections, dtype=jnp.int32)
    offset = jax.random.randint(key_off, (NYS,), 0, C_DEV, dtype=jnp.int32)
    return section * (C_DEV * groups) + owner * C_DEV + offset


def level_of(own_key, extent, split, low, largest):
    def one(dim, blocks):
        heights = jax.random.uniform(jax.random.fold_in(jax.random.fold_in(own_key, 6), dim), (blocks,), jnp.float32, low / len(split), largest / len(split))
        return jnp.repeat(jnp.exp(heights), extent[dim] // blocks).reshape((-1,) + (1,) * (len(extent) - dim - 1))

    loudness = one(*split[0])
    for cut in split[1:]:
        loudness = loudness * one(*cut)
    return loudness


def bell_draw(stream_key, dims, scale, reach, pieces=(), held_as=jnp.bfloat16):
    result = jax.random.normal(stream_key, dims, jnp.float32) * scale
    if len(pieces) > 0:
        result = level_of(stream_key, dims, pieces, -0.22, 0.18) * result
    return jnp.clip(result, min=-reach, max=reach).astype(held_as)


def setup_inputs(seed: int = 0) -> dict:
    key_of = jax.random.split(jax.random.key(seed), 9)
    train_feats = bell_draw(key_of[0], (POOL, D), (D ** -0.5), 0.26367188, ((0, 8),))
    train_targets = bell_draw(key_of[1], (POOL, C), 1.0, 6.0, ((0, 8),), jnp.float32)
    batch_idx = draw_batch_idx(jax.random.fold_in(key_of[8], 71), 0)
    centers = bell_draw(key_of[3], (CENTERS, D), (D ** -0.5), 0.26367188, ((0, 32),))
    weights = bell_draw(key_of[4], (CENTERS, C), CENTERS ** -0.5, 0.0234375, ((0, 32),))
    nys_idx = draw_nys_idx(jax.random.fold_in(key_of[8], 71), 0)
    eig_vecs = bell_draw(key_of[6], (NYS, K_EIG), (4 * K_EIG) ** -0.5, 0.25, ((0, 8),), jnp.float32)
    eig_scale = jnp.clip(jnp.exp(jax.random.uniform(key_of[7], (K_EIG,), jnp.float32, math.log(0.2), math.log(1.0))), 0.2, 1.0)
    return dict(train_feats=train_feats, train_targets=train_targets, batch_idx=batch_idx, centers=centers, weights=weights, nys_idx=nys_idx, eig_vecs=eig_vecs, eig_scale=eig_scale)


def kernel_block(feats, cent):
    cross = lax.dot_general(feats, cent, (((1,), (1,)), ((), ())), preferred_element_type=jnp.float32)
    row_sq = lax.optimization_barrier(jnp.sum(jnp.square(feats.astype(jnp.float32)), axis=1))
    cent_sq = lax.optimization_barrier(jnp.sum(jnp.square(cent.astype(jnp.float32)), axis=1))
    dist_sq = row_sq[:, None] + cent_sq[None, :] - 2.0 * cross
    length = 1.5 / jnp.sqrt(jnp.float32(D))
    return jnp.exp((1.4142 - jnp.sqrt(dist_sq)) / length).astype(jnp.bfloat16)

def reference(train_feats, train_targets, batch_idx, centers, weights, nys_idx, eig_vecs, eig_scale):
    feats = train_feats[batch_idx]
    targets = train_targets[batch_idx]
    blocks = CENTERS // C_DEV
    cent_blocks = centers.reshape(blocks, C_DEV, D)
    weight_blocks = weights.reshape(blocks, C_DEV, C)

    def pred_step(total, pair):
        kern = kernel_block(feats, pair[0])
        return (total + jnp.dot(kern, pair[1], preferred_element_type=jnp.float32), kern)
    pred, kern_all = lax.scan(pred_step, jnp.zeros((BATCH, C), jnp.float32), (cent_blocks, weight_blocks))
    residual = pred - targets
    res_bf = residual.astype(jnp.bfloat16)

    def grad_block(kern):
        return lax.dot_general(kern, res_bf, (((0,), (0,)), ((), ())), preferred_element_type=jnp.float32)
    grad = lax.map(grad_block, kern_all).reshape(CENTERS, C)
    coords = grad[nys_idx]
    proj = jnp.dot(eig_vecs.T, coords, precision=lax.Precision.HIGHEST)
    corr = jnp.dot(eig_vecs, eig_scale[:, None] * proj, precision=lax.Precision.HIGHEST)
    spread = jnp.zeros((CENTERS, C), jnp.float32).at[nys_idx].add(corr)
    update = 16.0 / BATCH * (grad - spread)
    new_weights = (weights.astype(jnp.float32) - update).astype(jnp.bfloat16)
    return (new_weights, residual)
```

```python
import math

import jax
import jax.numpy as jnp
from jax import lax
from jax.sharding import PartitionSpec as P

HIGH = lax.Precision.HIGHEST


def spread_out(rows, axes):
    count = lax.axis_size(axes)
    return lax.all_to_all(jnp.broadcast_to(rows[None], (count,) + rows.shape), axes, 0, 0, tiled=False)


def shards(train_feats, train_targets, batch_idx, centers, weights, nys_idx, eig_vecs, eig_scale):
    pool_rows = train_feats.shape[0]
    batch_rows = batch_idx.shape[0]
    center_rows = centers.shape[0]
    feat_dim = centers.shape[1]
    classes = weights.shape[1]
    wide_count = lax.axis_size("wide")
    sec_count = lax.axis_size("sec")
    wide_pos = lax.axis_index("wide")
    sec_pos = lax.axis_index("sec")
    batch_total = batch_rows * wide_count
    share_rows = batch_rows // sec_count
    local_rows = batch_idx - wide_pos * pool_rows
    picked = (local_rows[:, None] == jnp.arange(pool_rows)[None, :]).astype(jnp.bfloat16)
    my_feats = jnp.dot(picked, train_feats, preferred_element_type=jnp.float32).astype(jnp.bfloat16)
    piece = spread_out(my_feats, "wide")
    piece = jnp.transpose(piece, (1, 0, 2)).reshape(batch_total, feat_dim)
    my_targets = lax.dynamic_slice_in_dim(train_targets[local_rows], sec_pos * share_rows, share_rows, 0)

    nys_local = nys_idx % center_rows
    owned = nys_idx // (center_rows * wide_count) == sec_pos
    place = jnp.where(owned, nys_local, center_rows)
    hot = (place[None, :] == jnp.arange(center_rows)[:, None]).astype(jnp.float32)
    vecs = jnp.dot(hot, eig_vecs, precision=HIGH)

    cent_sq = jnp.sum(jnp.square(centers.astype(jnp.float32)), axis=1)
    length = 1.5 / math.sqrt(feat_dim)
    cross = lax.dot_general(
        piece, centers, (((1,), (1,)), ((), ())), preferred_element_type=jnp.float32
    )
    row_sq = jnp.sum(jnp.square(piece.astype(jnp.float32)), axis=1)
    dist_sq = row_sq[:, None] + cent_sq[None, :] - 2.0 * cross
    kern = jnp.exp((1.4142 - jnp.sqrt(dist_sq)) / length).astype(jnp.bfloat16)

    part = jnp.concatenate(
        [
            jnp.dot(kern, weights, preferred_element_type=jnp.float32),
            jnp.dot(kern.astype(jnp.float32), vecs, precision=HIGH),
        ],
        axis=1,
    )
    part = part.reshape(sec_count, share_rows, wide_count, -1).transpose(0, 2, 1, 3)
    part = part.reshape(sec_count * wide_count, share_rows, -1)
    mine = jnp.sum(lax.all_to_all(part, ("sec", "wide"), 0, 0, tiled=False), axis=0)
    mine = jnp.concatenate([mine[:, :classes] - my_targets, mine[:, classes:]], axis=1)
    both = spread_out(mine, ("sec", "wide")).reshape(sec_count, wide_count, share_rows, -1)
    both = both.transpose(0, 2, 1, 3).reshape(batch_rows, wide_count, -1)
    residual = lax.dynamic_index_in_dim(both[:, :, :classes], wide_pos, 1, keepdims=False)
    both = both.reshape(batch_total, -1)
    res_bf = both[:, :classes].astype(jnp.bfloat16)
    coords = both[:, classes:]

    drop = lax.dot_general(coords * eig_scale[None, :], vecs, (((1,), (1,)), ((), ())), precision=HIGH)
    drop_hi = drop.astype(jnp.bfloat16)
    drop_lo = (drop - drop_hi.astype(jnp.float32)).astype(jnp.bfloat16)
    factors = jnp.concatenate([kern, -drop_hi, -drop_lo], axis=0)
    grad = lax.dot_general(
        factors,
        jnp.concatenate([res_bf, res_bf, res_bf], axis=0),
        (((0,), (0,)), ((), ())),
        preferred_element_type=jnp.float32,
    )
    new_weights = (weights.astype(jnp.float32) - 16.0 / batch_total * grad).astype(jnp.bfloat16)
    return (new_weights, residual)


def solution(mesh):
    return jax.shard_map(
        shards,
        mesh=mesh,
        in_specs=(
            P("wide", None),
            P("wide", None),
            P("wide"),
            P(("sec", "wide"), None),
            P(("sec", "wide"), None),
            P("wide"),
            P("wide", None),
            P(),
        ),
        out_specs=(P(("sec", "wide"), None), P("wide", None)),
        check_vma=False,
    )
```

```python
import functools
import math

import jax
import jax.numpy as jnp
from jax import lax
from jax.experimental import pallas as pl
from jax.experimental.pallas import tpu as pltpu
from jax.sharding import PartitionSpec as P

VMEM_GRANT = 24 << 20
HIGH = lax.Precision.HIGHEST
NT = (((1,), (1,)), ((), ()))
NN = (((1,), (0,)), ((), ()))


def dot32(a, b, dims):
    return lax.dot_general(a, b, dims, preferred_element_type=jnp.float32)


def halves(x):
    top = x.astype(jnp.bfloat16)
    return top, (x - top.astype(jnp.float32)).astype(jnp.bfloat16)


def share_body(feats_ref, cents_ref, cent_sq_ref, wt_ref, vecs_ref, kern_ref, part_ref, *, step):
    center_rows, feat_dim = cents_ref.shape
    classes = wt_ref.shape[0]
    length = 1.5 / math.sqrt(feat_dim)
    feats = feats_ref[...]
    wide_feats = feats.astype(jnp.float32)
    row_sq = jnp.sum(wide_feats * wide_feats, axis=1, keepdims=True)
    for start in range(0, center_rows, step):
        cols = pl.ds(start, step)
        cross = dot32(feats, cents_ref[cols, :], NT)
        dist_sq = jnp.maximum(row_sq + cent_sq_ref[:, cols] - 2.0 * cross, 0.0)
        kern_ref[:, cols] = jnp.exp((1.4142 - jnp.sqrt(dist_sq)) / length).astype(jnp.bfloat16)
    kern = kern_ref[...]
    vec_hi, vec_lo = halves(vecs_ref[...])
    part_ref[:, 0, :classes] = dot32(kern, wt_ref[...], NT)
    part_ref[:, 0, classes:] = dot32(kern, vec_hi, NN) + dot32(kern, vec_lo, NN)


def update_body(pos_ref, both_ref, scale_ref, kern_ref, vecs_ref, wt_ref, out_ref, res_ref, left_ref, *, rate, sections):
    classes = wt_ref.shape[0]
    batch_total = both_ref.shape[0]
    wide_count = batch_total // sections

    @pl.when(pl.program_id(0) == 0)
    def _():
        turned = both_ref[:, 0, :classes].T.astype(jnp.bfloat16)
        left_ref[...] = jnp.concatenate([turned, turned, turned], axis=1)
        for s in range(sections):
            res_ref[s, :] = both_ref[s * wide_count + pos_ref[0], 0, :classes]

    coords_hi, coords_lo = halves(both_ref[:, 0, classes:] * scale_ref[...])
    vec_hi, vec_lo = halves(vecs_ref[...])
    drop = dot32(coords_hi, vec_hi, NT) + dot32(coords_hi, vec_lo, NT) + dot32(coords_lo, vec_hi, NT)
    drop_hi, drop_lo = halves(-drop)
    grad = dot32(left_ref[...], jnp.concatenate([kern_ref[...], drop_hi, drop_lo], axis=0), NN)
    out_ref[...] = (wt_ref[...].astype(jnp.float32) - rate * grad).astype(jnp.bfloat16)


def shards(train_feats, train_targets, batch_idx, centers, weights, nys_idx, eig_vecs, eig_scale):
    pool_rows = train_feats.shape[0]
    batch_rows = batch_idx.shape[0]
    center_rows, feat_dim = centers.shape
    classes = weights.shape[1]
    eig_count = eig_vecs.shape[1]
    wide_count = lax.axis_size("wide")
    sec_count = lax.axis_size("sec")
    wide_pos = lax.axis_index("wide")
    sec_pos = lax.axis_index("sec")
    batch_total = batch_rows * wide_count
    cols = classes + eig_count
    assert batch_rows == sec_count
    vmem = pl.BlockSpec(memory_space=pltpu.VMEM)

    local_rows = batch_idx - wide_pos * pool_rows
    picked = (local_rows[None, :, None] == jnp.arange(pool_rows)[None, None, :]).astype(jnp.bfloat16)
    picked = jnp.broadcast_to(picked, (wide_count, batch_rows, pool_rows))
    copies = lax.dot_general(picked, train_feats, (((2,), (0,)), ((), ())), preferred_element_type=jnp.float32)
    piece = lax.all_to_all(copies.astype(jnp.bfloat16), "wide", 0, 0, tiled=False)
    piece = jnp.transpose(piece, (1, 0, 2)).reshape(batch_total, feat_dim)
    my_target = lax.dynamic_slice_in_dim(train_targets[local_rows], sec_pos, 1, 0)

    owned = nys_idx // (center_rows * wide_count) == sec_pos
    place = jnp.where(owned, nys_idx % center_rows, center_rows)
    hot = (place[None, :] == jnp.arange(center_rows)[:, None]).astype(jnp.float32)
    vecs = jnp.dot(hot, eig_vecs, precision=HIGH)
    cent_sq = jnp.sum(jnp.square(centers.astype(jnp.float32)), axis=1)[None, :]

    turned_weights = weights.T
    kern, part = pl.pallas_call(
        functools.partial(share_body, step=min(512, center_rows)),
        out_shape=(
            jax.ShapeDtypeStruct((batch_total, center_rows), jnp.bfloat16),
            jax.ShapeDtypeStruct((batch_total, 1, cols), jnp.float32),
        ),
        in_specs=[vmem] * 5,
        out_specs=(vmem, vmem),
        compiler_params=pltpu.CompilerParams(vmem_limit_bytes=VMEM_GRANT),
        name="share",
    )(piece, centers, cent_sq, turned_weights, vecs)

    mine = jnp.sum(lax.all_to_all(part, ("sec", "wide"), 0, 0, tiled=False), axis=0)
    mine = jnp.concatenate([mine[:, :classes] - my_target, mine[:, classes:]], axis=1)
    both = lax.all_to_all(
        jnp.broadcast_to(mine[None], (batch_total, 1, cols)), ("sec", "wide"), 0, 0, tiled=False
    )

    block = min(256, center_rows)
    new_turned, residual = pl.pallas_call(
        functools.partial(update_body, rate=16.0 / batch_total, sections=sec_count),
        grid=(center_rows // block,),
        out_shape=(
            jax.ShapeDtypeStruct((classes, center_rows), jnp.bfloat16),
            jax.ShapeDtypeStruct((batch_rows, classes), jnp.float32),
        ),
        in_specs=[
            pl.BlockSpec(memory_space=pltpu.SMEM),
            pl.BlockSpec((batch_total, 1, cols), lambda i: (0, 0, 0)),
            pl.BlockSpec((1, eig_count), lambda i: (0, 0)),
            pl.BlockSpec((batch_total, block), lambda i: (0, i)),
            pl.BlockSpec((block, eig_count), lambda i: (i, 0)),
            pl.BlockSpec((classes, block), lambda i: (0, i)),
        ],
        out_specs=(
            pl.BlockSpec((classes, block), lambda i: (0, i)),
            pl.BlockSpec((batch_rows, classes), lambda i: (0, 0)),
        ),
        scratch_shapes=[pltpu.VMEM((classes, 3 * batch_total), jnp.bfloat16)],
        compiler_params=pltpu.CompilerParams(vmem_limit_bytes=VMEM_GRANT),
        name="update",
    )(wide_pos[None], both, eig_scale[None, :], kern, vecs, turned_weights)
    return (new_turned.T, residual)


def solution(mesh):
    return jax.shard_map(
        shards,
        mesh=mesh,
        in_specs=(
            P("wide", None),
            P("wide", None),
            P("wide"),
            P(("sec", "wide"), None),
            P(("sec", "wide"), None),
            P("wide"),
            P("wide", None),
            P(),
        ),
        out_specs=(P(("sec", "wide"), None), P("wide", None)),
        check_vma=False,
    )
```

```python
import functools
import math

import jax
import jax.numpy as jnp
from jax import lax
from jax.experimental import pallas as pl
from jax.experimental.pallas import tpu as pltpu
from jax.sharding import PartitionSpec as P

VMEM_GRANT = 16 << 20
NT = (((1,), (1,)), ((), ()))
NN = (((1,), (0,)), ((), ()))


def dot32(a, b, dims):
    return lax.dot_general(a, b, dims, preferred_element_type=jnp.float32)


def halves(x):
    top = x.astype(jnp.bfloat16)
    return top, (x - top.astype(jnp.float32)).astype(jnp.bfloat16)


def in_hbm(x):
    return pltpu.with_memory_space_constraint(x, pltpu.HBM)


def gather_body(pos_ref, idx_hbm, rows_hbm, out_ref, idx_ref, rows_ref, sems):
    get_idx = pltpu.make_async_copy(idx_hbm, idx_ref, sems.at[0])
    get_rows = pltpu.make_async_copy(rows_hbm, rows_ref, sems.at[1])
    get_idx.start()
    get_rows.start()
    get_idx.wait()
    pool_rows = rows_ref.shape[0]
    copies, batch_rows = out_ref.shape[:2]
    shape = (batch_rows, pool_rows)
    row = lax.broadcasted_iota(jnp.int32, shape, 0)
    wanted = jnp.zeros(shape, jnp.int32)
    for j in range(batch_rows):
        wanted = jnp.where(row == j, idx_ref[j] - pos_ref[0] * pool_rows, wanted)
    picked = (lax.broadcasted_iota(jnp.int32, shape, 1) == wanted).astype(jnp.bfloat16)
    get_rows.wait()
    rows = dot32(picked, rows_ref[...], NN).astype(jnp.bfloat16)
    for w in range(copies):
        out_ref[w] = rows


def stage_body(
    pos_ref, nys_hbm, eig_hbm, cents_hbm, cents_ref, cent_sq_ref, vecs_ref, nys_ref, eig_ref, sems, *, step
):
    pairs = ((nys_hbm, nys_ref), (eig_hbm, eig_ref), (cents_hbm, cents_ref))
    gets = [pltpu.make_async_copy(src, dst, sems.at[i]) for i, (src, dst) in enumerate(pairs)]
    for get in gets:
        get.start()
    gets[0].wait()
    gets[1].wait()
    center_rows = cents_ref.shape[0]
    nys_count = nys_ref.shape[1]
    eig_hi, eig_lo = halves(eig_ref[...])
    place = nys_ref[...] - pos_ref[0] * center_rows
    for start in range(0, center_rows, step):
        at = lax.broadcasted_iota(jnp.int32, (step, nys_count), 0) + start
        hot = (at == place).astype(jnp.bfloat16)
        vecs_ref[pl.ds(start, step), :] = dot32(hot, eig_hi, NN) + dot32(hot, eig_lo, NN)
    gets[2].wait()
    ones = jnp.ones((8, cents_ref.shape[1]), jnp.bfloat16)
    for start in range(0, center_rows, step):
        rows = cents_ref[pl.ds(start, step), :].astype(jnp.float32)
        top, low = halves(rows * rows)
        total = dot32(ones, top, NT) + dot32(ones, low, NT)
        cent_sq_ref[:, pl.ds(start, step)] = total[:1]


def fetch(src_hbm, dst_ref, sems, step):
    gets = []
    for i in range(src_hbm.shape[1] // step):
        cols = pl.ds(i * step, step)
        gets.append(pltpu.make_async_copy(src_hbm.at[:, cols], dst_ref.at[:, cols], sems.at[i]))
        gets[-1].start()
    return gets


def share_body(feats_ref, cents_ref, cent_sq_ref, vecs_ref, wt_hbm, kern_ref, part_ref, wt_ref, sems, *, step):
    gets = fetch(wt_hbm, wt_ref, sems, step)
    center_rows, feat_dim = cents_ref.shape
    classes = wt_ref.shape[0]
    length = 1.5 / math.sqrt(feat_dim)
    feats = feats_ref[...]
    wide_feats = feats.astype(jnp.float32)
    row_sq = jnp.sum(wide_feats * wide_feats, axis=1, keepdims=True)
    for start in range(0, center_rows, step):
        cols = pl.ds(start, step)
        cross = dot32(feats, cents_ref[cols, :], NT)
        dist_sq = jnp.maximum(row_sq + cent_sq_ref[:, cols] - 2.0 * cross, 0.0)
        kern_ref[:, cols] = jnp.exp((1.4142 - jnp.sqrt(dist_sq)) / length).astype(jnp.bfloat16)
    vec_hi, vec_lo = halves(vecs_ref[...])
    part_ref[:, 0, classes:] = dot32(kern_ref[...], vec_hi, NN) + dot32(kern_ref[...], vec_lo, NN)
    total = None
    for i, get in enumerate(gets):
        cols = pl.ds(i * step, step)
        get.wait()
        term = dot32(kern_ref[:, cols], wt_ref[:, cols], NT)
        total = term if total is None else total + term
    part_ref[:, 0, :classes] = total


def update_body(
    pos_ref, both_ref, scale_ref, kern_ref, vecs_ref, wt_hbm, out_hbm, res_ref,
    left_ref, wt_ref, new_ref, get_sems, put_sems, *, rate, sections, step
):
    gets = fetch(wt_hbm, wt_ref, get_sems, step)
    classes = wt_ref.shape[0]
    wide_count = both_ref.shape[0] // sections
    turned = both_ref[:, 0, :classes].T.astype(jnp.bfloat16)
    left_ref[...] = jnp.concatenate([turned, turned, turned], axis=1)
    coords_hi, coords_lo = halves(both_ref[:, 0, classes:] * scale_ref[...])
    puts = []
    for i, get in enumerate(gets):
        cols = pl.ds(i * step, step)
        vec_hi, vec_lo = halves(vecs_ref[cols, :])
        drop = dot32(coords_hi, vec_hi, NT) + dot32(coords_hi, vec_lo, NT) + dot32(coords_lo, vec_hi, NT)
        drop_hi, drop_lo = halves(-drop)
        grad = dot32(left_ref[...], jnp.concatenate([kern_ref[:, cols], drop_hi, drop_lo], axis=0), NN)
        get.wait()
        new_ref[:, cols] = (wt_ref[:, cols].astype(jnp.float32) - rate * grad).astype(jnp.bfloat16)
        puts.append(pltpu.make_async_copy(new_ref.at[:, cols], out_hbm.at[:, cols], put_sems.at[i]))
        puts[-1].start()
    for s in range(sections):
        res_ref[s, :] = both_ref[s * wide_count + pos_ref[0], 0, :classes]
    for put in puts:
        put.wait()


def shards(train_feats, train_targets, batch_idx, centers, weights, nys_idx, eig_vecs, eig_scale):
    pool_rows = train_feats.shape[0]
    batch_rows = batch_idx.shape[0]
    center_rows, feat_dim = centers.shape
    classes = weights.shape[1]
    eig_count = eig_vecs.shape[1]
    wide_count = lax.axis_size("wide")
    sec_count = lax.axis_size("sec")
    wide_pos = lax.axis_index("wide")
    sec_pos = lax.axis_index("sec")
    batch_total = batch_rows * wide_count
    cols = classes + eig_count
    assert batch_rows == sec_count
    vmem = pl.BlockSpec(memory_space=pltpu.VMEM)
    smem = pl.BlockSpec(memory_space=pltpu.SMEM)
    hbm = pl.BlockSpec(memory_space=pltpu.HBM)

    params = pltpu.CompilerParams(vmem_limit_bytes=VMEM_GRANT)
    step = min(512, center_rows)

    copies = pl.pallas_call(
        gather_body,
        out_shape=jax.ShapeDtypeStruct((wide_count, batch_rows, feat_dim), jnp.bfloat16),
        in_specs=[smem, hbm, hbm],
        out_specs=vmem,
        scratch_shapes=[
            pltpu.SMEM((batch_rows,), jnp.int32),
            pltpu.VMEM(train_feats.shape, train_feats.dtype),
            pltpu.SemaphoreType.DMA((2,)),
        ],
        compiler_params=params,
        name="gather",
    )(wide_pos[None], in_hbm(batch_idx), in_hbm(train_feats))
    piece = lax.all_to_all(copies, "wide", 0, 0, tiled=False)
    piece = jnp.transpose(piece, (1, 0, 2)).reshape(batch_total, feat_dim)
    my_target = lax.dynamic_slice_in_dim(train_targets[batch_idx - wide_pos * pool_rows], sec_pos, 1, 0)

    turned_weights = in_hbm(weights.T)
    staged_centers, cent_sq, vecs = pl.pallas_call(
        functools.partial(stage_body, step=step),
        out_shape=(
            jax.ShapeDtypeStruct(centers.shape, centers.dtype),
            jax.ShapeDtypeStruct((1, center_rows), jnp.float32),
            jax.ShapeDtypeStruct((center_rows, eig_count), jnp.float32),
        ),
        in_specs=[smem, hbm, hbm, hbm],
        out_specs=(vmem, vmem, vmem),
        scratch_shapes=[
            pltpu.VMEM((1, nys_idx.shape[0]), jnp.int32),
            pltpu.VMEM(eig_vecs.shape, jnp.float32),
            pltpu.SemaphoreType.DMA((3,)),
        ],
        compiler_params=params,
        cost_estimate=pl.CostEstimate(flops=1 << 31, bytes_accessed=16 << 20, transcendentals=0),
        name="stage",
    )(
        (sec_pos * wide_count + wide_pos)[None],
        in_hbm(nys_idx[None, :]),
        in_hbm(eig_vecs),
        in_hbm(centers),
    )

    slabs = center_rows // step
    kern, part = pl.pallas_call(
        functools.partial(share_body, step=step),
        out_shape=(
            jax.ShapeDtypeStruct((batch_total, center_rows), jnp.bfloat16),
            jax.ShapeDtypeStruct((batch_total, 1, cols), jnp.float32),
        ),
        in_specs=[vmem] * 4 + [hbm],
        out_specs=(vmem, vmem),
        scratch_shapes=[pltpu.VMEM((classes, center_rows), jnp.bfloat16), pltpu.SemaphoreType.DMA((slabs,))],
        compiler_params=params,
        name="share",
    )(piece, staged_centers, cent_sq, vecs, turned_weights)

    mine = jnp.sum(lax.all_to_all(part, ("sec", "wide"), 0, 0, tiled=False), axis=0)
    mine = jnp.concatenate([mine[:, :classes] - my_target, mine[:, classes:]], axis=1)
    both = lax.all_to_all(
        jnp.broadcast_to(mine[None], (batch_total, 1, cols)), ("sec", "wide"), 0, 0, tiled=False
    )

    new_turned, residual = pl.pallas_call(
        functools.partial(update_body, rate=16.0 / batch_total, sections=sec_count, step=step),
        out_shape=(
            jax.ShapeDtypeStruct((classes, center_rows), jnp.bfloat16),
            jax.ShapeDtypeStruct((batch_rows, classes), jnp.float32),
        ),
        in_specs=[smem] + [vmem] * 4 + [hbm],
        out_specs=(hbm, vmem),
        scratch_shapes=[
            pltpu.VMEM((classes, 3 * batch_total), jnp.bfloat16),
            pltpu.VMEM((classes, center_rows), jnp.bfloat16),
            pltpu.VMEM((classes, center_rows), jnp.bfloat16),
            pltpu.SemaphoreType.DMA((slabs,)),
            pltpu.SemaphoreType.DMA((slabs,)),
        ],
        compiler_params=params,
        name="update",
    )(wide_pos[None], both, eig_scale[None, :], kern, vecs, turned_weights)
    return (new_turned.T, residual)


def solution(mesh):
    return jax.shard_map(
        shards,
        mesh=mesh,
        in_specs=(
            P("wide", None),
            P("wide", None),
            P("wide"),
            P(("sec", "wide"), None),
            P(("sec", "wide"), None),
            P("wide"),
            P("wide", None),
            P(),
        ),
        out_specs=(P(("sec", "wide"), None), P("wide", None)),
        check_vma=False,
    )
```

```python
import functools
import math

import jax
import jax.numpy as jnp
from jax import lax
from jax.experimental import pallas as pl
from jax.experimental.pallas import tpu as pltpu
from jax.sharding import PartitionSpec as P

LANES = 128
VMEM_GRANT = 16 << 20
NT = (((1,), (1,)), ((), ()))
NN = (((1,), (0,)), ((), ()))


def dot32(a, b, dims):
    return lax.dot_general(a, b, dims, preferred_element_type=jnp.float32)


def halves(x):
    top = x.astype(jnp.bfloat16)
    return top, (x - top.astype(jnp.float32)).astype(jnp.bfloat16)


def in_hbm(x):
    return pltpu.with_memory_space_constraint(x, pltpu.HBM)


def gather_body(pos_ref, idx_hbm, rows_hbm, out_ref, idx_ref, rows_ref, sems):
    get_idx = pltpu.make_async_copy(idx_hbm, idx_ref, sems.at[0])
    get_rows = pltpu.make_async_copy(rows_hbm, rows_ref, sems.at[1])
    get_idx.start()
    get_rows.start()
    get_idx.wait()
    pool_rows = rows_ref.shape[0]
    copies, batch_rows = out_ref.shape[:2]
    shape = (batch_rows, pool_rows)
    row = lax.broadcasted_iota(jnp.int32, shape, 0)
    wanted = jnp.zeros(shape, jnp.int32)
    for j in range(batch_rows):
        wanted = jnp.where(row == j, idx_ref[j] - pos_ref[0] * pool_rows, wanted)
    picked = (lax.broadcasted_iota(jnp.int32, shape, 1) == wanted).astype(jnp.bfloat16)
    get_rows.wait()
    rows = dot32(picked, rows_ref[...], NN).astype(jnp.bfloat16)
    for w in range(copies):
        out_ref[w] = rows


def stage_body(
    pos_ref, nys_hbm, eig_hbm, idx_hbm, targets_hbm, cents_hbm, cents_ref, cent_sq_ref, vecs_ref, wanted_ref,
    nys_ref, eig_ref, idx_ref, targets_ref, sems, *, wide_count
):
    pairs = (
        (nys_hbm, nys_ref), (eig_hbm, eig_ref), (idx_hbm, idx_ref), (targets_hbm, targets_ref), (cents_hbm, cents_ref)
    )
    gets = [pltpu.make_async_copy(src, dst, sems.at[i]) for i, (src, dst) in enumerate(pairs)]
    for get in gets:
        get.start()
    gets[0].wait()
    gets[1].wait()
    center_rows, feat_dim = cents_ref.shape
    nys_count, eig_count = eig_ref.shape
    eig_both = jnp.concatenate(halves(eig_ref[...]), axis=1)
    place = nys_ref[...] - pos_ref[0] * center_rows
    for start in range(0, center_rows, LANES):
        rows = pl.ds(start, LANES)
        at = lax.broadcasted_iota(jnp.int32, (LANES, nys_count), 0) + start
        moved = dot32((at == place).astype(jnp.bfloat16), eig_both, NN)
        vec_hi, vec_lo = halves(moved[:, :eig_count] + moved[:, eig_count:])
        vecs_ref[rows, :eig_count] = vec_hi
        vecs_ref[rows, eig_count:] = vec_lo
    gets[2].wait()
    gets[3].wait()
    pool_rows, classes = targets_ref.shape
    row = idx_ref[pos_ref[0] // wide_count] - pos_ref[0] % wide_count * pool_rows
    wanted_ref[...] = jnp.zeros_like(wanted_ref)
    wanted_ref[:, pl.ds(eig_count, classes)] = targets_ref[pl.ds(row, 1), :]
    gets[4].wait()
    for start in range(0, center_rows, LANES):
        total = jnp.zeros((LANES, LANES), jnp.float32)
        for lane in range(0, feat_dim, LANES):
            part = cents_ref[pl.ds(start, LANES), pl.ds(lane, LANES)].astype(jnp.float32)
            total = total + part * part
        cent_sq_ref[:, pl.ds(start, LANES)] = jnp.sum(total.T, axis=0, keepdims=True)


def fetch(src_hbm, dst_ref, sems, step):
    gets = []
    for i in range(src_hbm.shape[1] // step):
        cols = pl.ds(i * step, step)
        gets.append(pltpu.make_async_copy(src_hbm.at[:, cols], dst_ref.at[:, cols], sems.at[i]))
        gets[-1].start()
    return gets


def lanes(ref, row, count, tile, tiles):
    return ref.at[pl.ds(row * tiles + tile, count, stride=tiles), :]


def share_body(pos_ref, feats_ref, cents_ref, cent_sq_ref, vecs_ref, wt_hbm, kern_ref, part_ref, wt_ref, sems, *, step):
    gets = fetch(wt_hbm, wt_ref, sems, step)

    @pl.when(pos_ref[0] >= 0)
    def _():
        batch_total = feats_ref.shape[0]
        center_rows, feat_dim = cents_ref.shape
        classes = wt_ref.shape[0]
        eig_count = vecs_ref.shape[1] // 2
        tiles = part_ref.shape[0] // batch_total
        length = 1.5 / math.sqrt(feat_dim)
        feats = feats_ref[...]
        wide_feats = feats.astype(jnp.float32)
        row_sq = jnp.sum(wide_feats * wide_feats, axis=1, keepdims=True)
        for start in range(0, center_rows, step):
            cols = pl.ds(start, step)
            cross = dot32(feats, cents_ref[cols, :], NT)
            dist_sq = jnp.maximum(row_sq + cent_sq_ref[:, cols] - 2.0 * cross, 0.0)
            kern_ref[:, cols] = jnp.exp((1.4142 - jnp.sqrt(dist_sq)) / length).astype(jnp.bfloat16)
        coords = dot32(kern_ref[...], vecs_ref[...], NN)
        coords = coords[:, :eig_count] + coords[:, eig_count:]
        total = None
        for i, get in enumerate(gets):
            cols = pl.ds(i * step, step)
            get.wait()
            term = dot32(kern_ref[:, cols], wt_ref[:, cols], NT)
            total = term if total is None else total + term
        pad = jnp.zeros((batch_total, tiles * LANES - eig_count - classes), jnp.float32)
        part = jnp.concatenate([coords, total, pad], axis=1)
        for tile in range(tiles):
            for row in range(0, batch_total, 8):
                lanes(part_ref, row, 8, tile, tiles)[...] = part[row : row + 8, tile * LANES : (tile + 1) * LANES]


def update_body(
    pos_ref, both_ref, scale_ref, kern_ref, vecs_ref, wt_hbm, out_hbm, res_ref,
    left_ref, wt_ref, new_ref, get_sems, put_sems, *, rate, sections, step, chunk
):
    gets = fetch(wt_hbm, wt_ref, get_sems, step)
    fold = math.frexp(rate)[0] == 0.5
    classes = wt_ref.shape[0]
    batch_total = kern_ref.shape[0]
    eig_count = vecs_ref.shape[1] // 2
    first = eig_count // LANES
    tiles = both_ref.shape[0] // batch_total
    wide_count = batch_total // sections
    for tile in range(first, tiles):
        rows = lanes(both_ref, 0, batch_total, tile, tiles)[...].astype(jnp.bfloat16)
        if fold:
            rows = (rows.astype(jnp.float32) * rate).astype(jnp.bfloat16)
        turned = jnp.concatenate([rows, rows, rows, rows], axis=0).T
        left_ref[pl.ds((tile - first) * LANES, LANES), :] = turned
    coords = jnp.concatenate([lanes(both_ref, 0, batch_total, tile, tiles)[...] for tile in range(first)], axis=1)
    coords_hi, coords_lo = halves(coords * scale_ref[...])
    both_hi = jnp.concatenate([coords_hi, coords_hi], axis=1)
    puts = []
    for i, get in enumerate(gets):
        cols = pl.ds(i * step, step)
        vecs = vecs_ref[cols, :]
        drop = dot32(both_hi, vecs, NT) + dot32(coords_lo, vecs[:, :eig_count], NT)
        drop_hi, drop_lo = halves(-drop)
        factors = jnp.concatenate([kern_ref[:, cols], drop_hi, drop_lo, jnp.zeros_like(drop_lo)], axis=0)
        get.wait()
        for row in range(0, classes, chunk):
            part = pl.ds(row, min(chunk, classes - row))
            grad = dot32(left_ref[part, :], factors, NN)
            grad = grad if fold else rate * grad
            new_ref[part, cols] = (wt_ref[part, cols].astype(jnp.float32) - grad).astype(jnp.bfloat16)
        puts.append(pltpu.make_async_copy(new_ref.at[:, cols], out_hbm.at[:, cols], put_sems.at[i]))
        puts[-1].start()
    for s in range(sections):
        for tile in range(first, tiles):
            width = min(LANES, classes - (tile - first) * LANES)
            row = lanes(both_ref, s * wide_count + pos_ref[0], 1, tile, tiles)[...]
            res_ref[pl.ds(s, 1), pl.ds((tile - first) * LANES, width)] = row[:, :width]
    for put in puts:
        put.wait()


def shards(train_feats, train_targets, batch_idx, centers, weights, nys_idx, eig_vecs, eig_scale):
    batch_rows = batch_idx.shape[0]
    center_rows, feat_dim = centers.shape
    classes = weights.shape[1]
    eig_count = eig_vecs.shape[1]
    wide_count = lax.axis_size("wide")
    sec_count = lax.axis_size("sec")
    wide_pos = lax.axis_index("wide")
    sec_pos = lax.axis_index("sec")
    batch_total = batch_rows * wide_count
    tiles = eig_count // LANES + pl.cdiv(classes, LANES)
    assert batch_rows == sec_count and eig_count % LANES == 0
    vmem = pl.BlockSpec(memory_space=pltpu.VMEM)
    smem = pl.BlockSpec(memory_space=pltpu.SMEM)
    hbm = pl.BlockSpec(memory_space=pltpu.HBM)

    params = pltpu.CompilerParams(vmem_limit_bytes=VMEM_GRANT)
    step = min(512, center_rows)

    copies = pl.pallas_call(
        gather_body,
        out_shape=jax.ShapeDtypeStruct((wide_count, batch_rows, feat_dim), jnp.bfloat16),
        in_specs=[smem, hbm, hbm],
        out_specs=vmem,
        scratch_shapes=[
            pltpu.SMEM((batch_rows,), jnp.int32),
            pltpu.VMEM(train_feats.shape, train_feats.dtype),
            pltpu.SemaphoreType.DMA((2,)),
        ],
        compiler_params=params,
        name="gather",
    )(wide_pos[None], in_hbm(batch_idx), in_hbm(train_feats))
    piece = lax.all_to_all(copies, "wide", 0, 0, tiled=False)
    piece = jnp.transpose(piece, (1, 0, 2)).reshape(batch_total, feat_dim)

    turned_weights = in_hbm(weights.T)
    staged_centers, cent_sq, vecs, wanted = pl.pallas_call(
        functools.partial(stage_body, wide_count=wide_count),
        out_shape=(
            jax.ShapeDtypeStruct(centers.shape, centers.dtype),
            jax.ShapeDtypeStruct((1, center_rows), jnp.float32),
            jax.ShapeDtypeStruct((center_rows, 2 * eig_count), jnp.bfloat16),
            jax.ShapeDtypeStruct((1, tiles * LANES), jnp.float32),
        ),
        in_specs=[smem] + [hbm] * 5,
        out_specs=(vmem,) * 4,
        scratch_shapes=[
            pltpu.VMEM((1, nys_idx.shape[0]), jnp.int32),
            pltpu.VMEM(eig_vecs.shape, jnp.float32),
            pltpu.SMEM((batch_rows,), jnp.int32),
            pltpu.VMEM(train_targets.shape, jnp.float32),
            pltpu.SemaphoreType.DMA((5,)),
        ],
        compiler_params=params,
        cost_estimate=pl.CostEstimate(flops=1 << 31, bytes_accessed=16 << 20, transcendentals=0),
        name="stage",
    )(
        (sec_pos * wide_count + wide_pos)[None],
        in_hbm(nys_idx[None, :]),
        in_hbm(eig_vecs),
        in_hbm(batch_idx),
        in_hbm(train_targets),
        in_hbm(centers),
    )

    slabs = center_rows // step
    kern, part = pl.pallas_call(
        functools.partial(share_body, step=step),
        out_shape=(
            jax.ShapeDtypeStruct((batch_total, center_rows), jnp.bfloat16),
            jax.ShapeDtypeStruct((batch_total * tiles, LANES), jnp.float32),
        ),
        in_specs=[smem] + [vmem] * 4 + [hbm],
        out_specs=(vmem, vmem),
        scratch_shapes=[pltpu.VMEM((classes, center_rows), jnp.bfloat16), pltpu.SemaphoreType.DMA((slabs,))],
        compiler_params=params,
        name="share",
    )(wide_pos[None], piece, staged_centers, cent_sq, vecs, turned_weights)

    part = lax.all_to_all(part.reshape(batch_total, 1, tiles * LANES), ("sec", "wide"), 0, 0, tiled=False)
    mine = jnp.sum(part, axis=0) - wanted
    both = lax.all_to_all(jnp.broadcast_to(mine[None], part.shape), ("sec", "wide"), 0, 0, tiled=False)
    both = both.reshape(batch_total * tiles, LANES)

    new_turned, residual = pl.pallas_call(
        functools.partial(update_body, rate=16.0 / batch_total, sections=sec_count, step=step, chunk=128),
        out_shape=(
            jax.ShapeDtypeStruct((classes, center_rows), jnp.bfloat16),
            jax.ShapeDtypeStruct((batch_rows, classes), jnp.float32),
        ),
        in_specs=[smem] + [vmem] * 4 + [hbm],
        out_specs=(hbm, vmem),
        scratch_shapes=[
            pltpu.VMEM((pl.cdiv(classes, LANES) * LANES, 4 * batch_total), jnp.bfloat16),
            pltpu.VMEM((classes, center_rows), jnp.bfloat16),
            pltpu.VMEM((classes, center_rows), jnp.bfloat16),
            pltpu.SemaphoreType.DMA((slabs,)),
            pltpu.SemaphoreType.DMA((slabs,)),
        ],
        compiler_params=params,
        name="update",
    )(wide_pos[None], both, eig_scale[None, :], kern, vecs, turned_weights)
    return (new_turned.T, residual)


def solution(mesh):
    return jax.shard_map(
        shards,
        mesh=mesh,
        in_specs=(
            P("wide", None),
            P("wide", None),
            P("wide"),
            P(("sec", "wide"), None),
            P(("sec", "wide"), None),
            P("wide"),
            P("wide", None),
            P(),
        ),
        out_specs=(P(("sec", "wide"), None), P("wide", None)),
        check_vma=False,
    )
```

```python
import functools
import math

import jax
import jax.numpy as jnp
from jax import lax
from jax.experimental import pallas as pl
from jax.experimental.pallas import tpu as pltpu
from jax.sharding import PartitionSpec as P

LANES = 128
VMEM_GRANT = 16 << 20
NT = (((1,), (1,)), ((), ()))
NN = (((1,), (0,)), ((), ()))


def dot32(a, b, dims):
    return lax.dot_general(a, b, dims, preferred_element_type=jnp.float32)


def halves(x):
    top = x.astype(jnp.bfloat16)
    return top, (x - top.astype(jnp.float32)).astype(jnp.bfloat16)


def in_hbm(x):
    return pltpu.with_memory_space_constraint(x, pltpu.HBM)


def gather_body(pos_ref, idx_hbm, rows_hbm, out_ref, idx_ref, rows_ref, sems):
    get_idx = pltpu.make_async_copy(idx_hbm, idx_ref, sems.at[0])
    get_rows = pltpu.make_async_copy(rows_hbm, rows_ref, sems.at[1])
    get_idx.start()
    get_rows.start()
    get_idx.wait()
    pool_rows = rows_ref.shape[0]
    copies, batch_rows = out_ref.shape[:2]
    shape = (batch_rows, pool_rows)
    row = lax.broadcasted_iota(jnp.int32, shape, 0)
    wanted = jnp.zeros(shape, jnp.int32)
    for j in range(batch_rows):
        wanted = jnp.where(row == j, idx_ref[j] - pos_ref[0] * pool_rows, wanted)
    picked = (lax.broadcasted_iota(jnp.int32, shape, 1) == wanted).astype(jnp.bfloat16)
    get_rows.wait()
    rows = dot32(picked, rows_ref[...], NN).astype(jnp.bfloat16)
    for w in range(copies):
        out_ref[w] = rows


def stage_body(
    pos_ref, nys_hbm, eig_hbm, idx_hbm, targets_hbm, cents_hbm, cents_ref, cent_sq_ref, vecs_ref, wanted_ref,
    nys_ref, eig_ref, idx_ref, targets_ref, sems, *, wide_count
):
    pairs = (
        (nys_hbm, nys_ref), (eig_hbm, eig_ref), (idx_hbm, idx_ref), (targets_hbm, targets_ref), (cents_hbm, cents_ref)
    )
    gets = [pltpu.make_async_copy(src, dst, sems.at[i]) for i, (src, dst) in enumerate(pairs)]
    for get in gets:
        get.start()
    gets[0].wait()
    gets[1].wait()
    center_rows, feat_dim = cents_ref.shape
    nys_count, eig_count = eig_ref.shape
    eig_both = jnp.concatenate(halves(eig_ref[...]), axis=1)
    place = nys_ref[...] - pos_ref[0] * center_rows
    for start in range(0, center_rows, LANES):
        rows = pl.ds(start, LANES)
        at = lax.broadcasted_iota(jnp.int32, (LANES, nys_count), 0) + start
        moved = dot32((at == place).astype(jnp.bfloat16), eig_both, NN)
        vec_hi, vec_lo = halves(moved[:, :eig_count] + moved[:, eig_count:])
        vecs_ref[rows, :eig_count] = vec_hi
        vecs_ref[rows, eig_count:] = vec_lo
    gets[2].wait()
    gets[3].wait()
    pool_rows, classes = targets_ref.shape
    row = idx_ref[pos_ref[0] // wide_count] - pos_ref[0] % wide_count * pool_rows
    wanted_ref[...] = jnp.zeros_like(wanted_ref)
    wanted_ref[:, pl.ds(eig_count, classes)] = targets_ref[pl.ds(row, 1), :]
    gets[4].wait()
    for start in range(0, center_rows, LANES):
        total = jnp.zeros((LANES, LANES), jnp.float32)
        for lane in range(0, feat_dim, LANES):
            part = cents_ref[pl.ds(start, LANES), pl.ds(lane, LANES)].astype(jnp.float32)
            total = total + part * part
        cent_sq_ref[:, pl.ds(start, LANES)] = jnp.sum(total.T, axis=0, keepdims=True)


def lanes(ref, row, count, tile, tiles):
    return ref.at[pl.ds(row * tiles + tile, count, stride=tiles), :]


def share_body(pos_ref, feats_ref, cents_ref, cent_sq_ref, vecs_ref, wt_hbm, kern_ref, part_ref, wt_ref, sems, *, step):
    gets = []
    for i in range(wt_hbm.shape[1] // step):
        cols = pl.ds(i * step, step)
        gets.append(pltpu.make_async_copy(wt_hbm.at[:, cols], wt_ref.at[:, cols], sems.at[i]))
        gets[-1].start()

    @pl.when(pos_ref[0] >= 0)
    def _():
        batch_total = feats_ref.shape[0]
        center_rows, feat_dim = cents_ref.shape
        classes = wt_ref.shape[0]
        eig_count = vecs_ref.shape[1] // 2
        tiles = part_ref.shape[0] // batch_total
        length = 1.5 / math.sqrt(feat_dim)
        feats = feats_ref[...]
        wide_feats = feats.astype(jnp.float32)
        row_sq = jnp.sum(wide_feats * wide_feats, axis=1, keepdims=True)
        for start in range(0, center_rows, step):
            cols = pl.ds(start, step)
            cross = dot32(feats, cents_ref[cols, :], NT)
            dist_sq = jnp.maximum(row_sq + cent_sq_ref[:, cols] - 2.0 * cross, 0.0)
            kern_ref[:, cols] = jnp.exp((1.4142 - jnp.sqrt(dist_sq)) / length).astype(jnp.bfloat16)
        coords = dot32(kern_ref[...], vecs_ref[...], NN)
        coords = coords[:, :eig_count] + coords[:, eig_count:]
        total = None
        for i, get in enumerate(gets):
            cols = pl.ds(i * step, step)
            get.wait()
            term = dot32(kern_ref[:, cols], wt_ref[:, cols], NT)
            total = term if total is None else total + term
        pad = jnp.zeros((batch_total, tiles * LANES - eig_count - classes), jnp.float32)
        part = jnp.concatenate([coords, total, pad], axis=1)
        for tile in range(tiles):
            for row in range(0, batch_total, 8):
                lanes(part_ref, row, 8, tile, tiles)[...] = part[row : row + 8, tile * LANES : (tile + 1) * LANES]


def settle_body(parts_ref, wanted_ref, both_ref, *, count):
    tiles = parts_ref.shape[0] // count
    for tile in range(tiles):
        total = jnp.sum(lanes(parts_ref, 0, count, tile, tiles)[...], axis=0, keepdims=True)
        total = total - wanted_ref[:, tile * LANES : (tile + 1) * LANES]
        lanes(both_ref, 0, count, tile, tiles)[...] = jnp.broadcast_to(total, (count, LANES))


def update_body(
    pos_ref, both_ref, scale_ref, kern_ref, vecs_ref, wt_ref, out_hbm, res_hbm,
    left_ref, factors_ref, new_ref, res_ref, sems, *, rate, sections, step, chunk
):
    fold = math.frexp(rate)[0] == 0.5
    classes = wt_ref.shape[0]
    batch_total = kern_ref.shape[0]
    eig_count = vecs_ref.shape[1] // 2
    first = eig_count // LANES
    tiles = both_ref.shape[0] // batch_total
    wide_count = batch_total // sections
    for tile in range(first, tiles):
        rows = lanes(both_ref, 0, batch_total, tile, tiles)[...].astype(jnp.bfloat16)
        if fold:
            rows = (rows.astype(jnp.float32) * rate).astype(jnp.bfloat16)
        turned = jnp.concatenate([rows, rows, rows, rows], axis=0).T
        left_ref[pl.ds((tile - first) * LANES, LANES), :] = turned
    coords = jnp.concatenate([lanes(both_ref, 0, batch_total, tile, tiles)[...] for tile in range(first)], axis=1)
    coords_hi, coords_lo = halves(coords * scale_ref[...])
    coords = jnp.concatenate([coords_hi, coords_lo], axis=0)
    coords = jnp.concatenate([coords, coords], axis=1)
    for start in range(0, wt_ref.shape[1], step):
        cols = pl.ds(start, step)
        drop = dot32(coords, vecs_ref[cols, :], NT)
        drop = drop[:batch_total] + drop[batch_total:]
        drop_hi, drop_lo = halves(-drop)
        factors_ref[:, cols] = jnp.concatenate([kern_ref[:, cols], drop_hi, drop_lo, jnp.zeros_like(drop_lo)], axis=0)
    puts = []
    for start in range(0, wt_ref.shape[1], step):
        cols = pl.ds(start, step)
        factors = factors_ref[:, cols]
        for row in range(0, classes, chunk):
            part = pl.ds(row, min(chunk, classes - row))
            grad = dot32(left_ref[part, :], factors, NN)
            grad = grad if fold else rate * grad
            new_ref[part, cols] = (wt_ref[part, cols].astype(jnp.float32) - grad).astype(jnp.bfloat16)
            if row // chunk % 2 == 1 or row + chunk >= classes:
                rows = pl.ds(row // chunk // 2 * 2 * chunk, row % (2 * chunk) + part.size)
                spot = (rows, cols)
                puts.append(pltpu.make_async_copy(new_ref.at[spot], out_hbm.at[spot], sems.at[len(puts)]))
                puts[-1].start()
        if start == 0:
            for s in range(sections):
                for tile in range(first, tiles):
                    width = min(LANES, classes - (tile - first) * LANES)
                    row = lanes(both_ref, s * wide_count + pos_ref[0], 1, tile, tiles)[...]
                    res_ref[pl.ds(s, 1), pl.ds((tile - first) * LANES, width)] = row[:, :width]
            puts.append(pltpu.make_async_copy(res_ref, res_hbm, sems.at[len(puts)]))
            puts[-1].start()
    for put in puts:
        put.wait()


def shards(train_feats, train_targets, batch_idx, centers, weights, nys_idx, eig_vecs, eig_scale):
    batch_rows = batch_idx.shape[0]
    center_rows, feat_dim = centers.shape
    classes = weights.shape[1]
    eig_count = eig_vecs.shape[1]
    wide_count = lax.axis_size("wide")
    sec_count = lax.axis_size("sec")
    wide_pos = lax.axis_index("wide")
    sec_pos = lax.axis_index("sec")
    batch_total = batch_rows * wide_count
    tiles = eig_count // LANES + pl.cdiv(classes, LANES)
    assert batch_rows == sec_count and eig_count % LANES == 0
    vmem = pl.BlockSpec(memory_space=pltpu.VMEM)
    smem = pl.BlockSpec(memory_space=pltpu.SMEM)
    hbm = pl.BlockSpec(memory_space=pltpu.HBM)

    params = pltpu.CompilerParams(vmem_limit_bytes=VMEM_GRANT)
    step = min(512, center_rows // 4)
    chunk = LANES

    copies = pl.pallas_call(
        gather_body,
        out_shape=jax.ShapeDtypeStruct((wide_count, batch_rows, feat_dim), jnp.bfloat16),
        in_specs=[smem, hbm, hbm],
        out_specs=vmem,
        scratch_shapes=[
            pltpu.SMEM((batch_rows,), jnp.int32),
            pltpu.VMEM(train_feats.shape, train_feats.dtype),
            pltpu.SemaphoreType.DMA((2,)),
        ],
        compiler_params=params,
        name="gather",
    )(wide_pos[None], in_hbm(batch_idx), in_hbm(train_feats))
    piece = lax.all_to_all(copies, "wide", 0, 0, tiled=False)
    piece = jnp.transpose(piece, (1, 0, 2)).reshape(batch_total, feat_dim)

    turned_weights = in_hbm(weights.T)
    staged_centers, cent_sq, vecs, wanted = pl.pallas_call(
        functools.partial(stage_body, wide_count=wide_count),
        out_shape=(
            jax.ShapeDtypeStruct(centers.shape, centers.dtype),
            jax.ShapeDtypeStruct((1, center_rows), jnp.float32),
            jax.ShapeDtypeStruct((center_rows, 2 * eig_count), jnp.bfloat16),
            jax.ShapeDtypeStruct((1, tiles * LANES), jnp.float32),
        ),
        in_specs=[smem] + [hbm] * 5,
        out_specs=(vmem,) * 4,
        scratch_shapes=[
            pltpu.VMEM((1, nys_idx.shape[0]), jnp.int32),
            pltpu.VMEM(eig_vecs.shape, jnp.float32),
            pltpu.SMEM((batch_rows,), jnp.int32),
            pltpu.VMEM(train_targets.shape, jnp.float32),
            pltpu.SemaphoreType.DMA((5,)),
        ],
        compiler_params=params,
        cost_estimate=pl.CostEstimate(flops=1 << 31, bytes_accessed=16 << 20, transcendentals=0),
        name="stage",
    )(
        (sec_pos * wide_count + wide_pos)[None],
        in_hbm(nys_idx[None, :]),
        in_hbm(eig_vecs),
        in_hbm(batch_idx),
        in_hbm(train_targets),
        in_hbm(centers),
    )

    slab_count = center_rows // step
    kern, part, kept = pl.pallas_call(
        functools.partial(share_body, step=step),
        out_shape=(
            jax.ShapeDtypeStruct((batch_total, center_rows), jnp.bfloat16),
            jax.ShapeDtypeStruct((batch_total * tiles, LANES), jnp.float32),
            jax.ShapeDtypeStruct((classes, center_rows), jnp.bfloat16),
        ),
        in_specs=[smem] + [vmem] * 4 + [hbm],
        out_specs=(vmem, vmem, vmem),
        scratch_shapes=[pltpu.SemaphoreType.DMA((slab_count,))],
        compiler_params=params,
        name="share",
    )(wide_pos[None], piece, staged_centers, cent_sq, vecs, turned_weights)

    parts = lax.all_to_all(part.reshape(batch_total, 1, tiles * LANES), ("sec", "wide"), 0, 0, tiled=False)
    both = pl.pallas_call(
        functools.partial(settle_body, count=batch_total),
        out_shape=jax.ShapeDtypeStruct((batch_total * tiles, LANES), jnp.float32),
        in_specs=[vmem, vmem],
        out_specs=vmem,
        compiler_params=params,
        name="settle",
    )(parts.reshape(batch_total * tiles, LANES), wanted)
    both = lax.all_to_all(both.reshape(batch_total, 1, tiles * LANES), ("sec", "wide"), 0, 0, tiled=False)
    both = both.reshape(batch_total * tiles, LANES)

    new_turned, residual = pl.pallas_call(
        functools.partial(update_body, rate=16.0 / batch_total, sections=sec_count, step=step, chunk=chunk),
        out_shape=(
            jax.ShapeDtypeStruct((classes, center_rows), jnp.bfloat16),
            jax.ShapeDtypeStruct((batch_rows, classes), jnp.float32),
        ),
        in_specs=[smem] + [vmem] * 5,
        out_specs=(hbm, hbm),
        scratch_shapes=[
            pltpu.VMEM((pl.cdiv(classes, LANES) * LANES, 4 * batch_total), jnp.bfloat16),
            pltpu.VMEM((4 * batch_total, center_rows), jnp.bfloat16),
            pltpu.VMEM((classes, center_rows), jnp.bfloat16),
            pltpu.VMEM((batch_rows, classes), jnp.float32),
            pltpu.SemaphoreType.DMA((1 + slab_count * pl.cdiv(classes, 2 * chunk),)),
        ],
        compiler_params=params,
        name="update",
    )(wide_pos[None], both, eig_scale[None, :], kern, vecs, kept)
    return (new_turned.T, residual)


def solution(mesh):
    return jax.shard_map(
        shards,
        mesh=mesh,
        in_specs=(
            P("wide", None),
            P("wide", None),
            P("wide"),
            P(("sec", "wide"), None),
            P(("sec", "wide"), None),
            P("wide"),
            P("wide", None),
            P(),
        ),
        out_specs=(P(("sec", "wide"), None), P("wide", None)),
        check_vma=False,
    )
```

```python
import functools
import math

import jax
import jax.numpy as jnp
from jax import lax
from jax.experimental import pallas as pl
from jax.experimental.pallas import tpu as pltpu
from jax.sharding import PartitionSpec as P

LANES = 128
VMEM_GRANT = 16 << 20
NT = (((1,), (1,)), ((), ()))
NN = (((1,), (0,)), ((), ()))


def dot32(a, b, dims):
    return lax.dot_general(a, b, dims, preferred_element_type=jnp.float32)


def halves(x):
    top = x.astype(jnp.bfloat16)
    return top, (x - top.astype(jnp.float32)).astype(jnp.bfloat16)


def in_hbm(x):
    return pltpu.with_memory_space_constraint(x, pltpu.HBM)


def gather_body(pos_ref, idx_hbm, rows_hbm, out_ref, idx_ref, rows_ref, sems):
    get_idx = pltpu.make_async_copy(idx_hbm, idx_ref, sems.at[0])
    get_rows = pltpu.make_async_copy(rows_hbm, rows_ref, sems.at[1])
    get_idx.start()
    get_rows.start()
    get_idx.wait()
    pool_rows = rows_ref.shape[0]
    copies, batch_rows = out_ref.shape[:2]
    shape = (batch_rows, pool_rows)
    row = lax.broadcasted_iota(jnp.int32, shape, 0)
    wanted = jnp.zeros(shape, jnp.int32)
    for j in range(batch_rows):
        wanted = jnp.where(row == j, idx_ref[j] - pos_ref[0] * pool_rows, wanted)
    picked = (lax.broadcasted_iota(jnp.int32, shape, 1) == wanted).astype(jnp.bfloat16)
    get_rows.wait()
    rows = dot32(picked, rows_ref[...], NN).astype(jnp.bfloat16)
    for w in range(copies):
        out_ref[w] = rows


def stage_body(
    pos_ref, nys_hbm, eig_hbm, idx_hbm, targets_hbm, cents_hbm, cents_ref, cent_sq_ref, vecs_ref, wanted_ref,
    nys_ref, eig_ref, idx_ref, targets_ref, sems, *, wide_count
):
    pairs = (
        (nys_hbm, nys_ref), (eig_hbm, eig_ref), (idx_hbm, idx_ref), (targets_hbm, targets_ref), (cents_hbm, cents_ref)
    )
    gets = [pltpu.make_async_copy(src, dst, sems.at[i]) for i, (src, dst) in enumerate(pairs)]
    for get in gets:
        get.start()
    gets[0].wait()
    gets[1].wait()
    center_rows, feat_dim = cents_ref.shape
    nys_count, eig_count = eig_ref.shape
    eig_both = jnp.concatenate(halves(eig_ref[...]), axis=1)
    place = nys_ref[...] - pos_ref[0] * center_rows
    for start in range(0, center_rows, LANES):
        rows = pl.ds(start, LANES)
        at = lax.broadcasted_iota(jnp.int32, (LANES, nys_count), 0) + start
        moved = dot32((at == place).astype(jnp.bfloat16), eig_both, NN)
        vec_hi, vec_lo = halves(moved[:, :eig_count] + moved[:, eig_count:])
        vecs_ref[rows, :eig_count] = vec_hi
        vecs_ref[rows, eig_count:] = vec_lo
    gets[2].wait()
    gets[3].wait()
    pool_rows, classes = targets_ref.shape
    row = idx_ref[pos_ref[0] // wide_count] - pos_ref[0] % wide_count * pool_rows
    wanted_ref[...] = jnp.zeros_like(wanted_ref)
    wanted_ref[:, pl.ds(eig_count, classes)] = targets_ref[pl.ds(row, 1), :]
    gets[4].wait()
    for start in range(0, center_rows, LANES):
        total = jnp.zeros((LANES, LANES), jnp.float32)
        for lane in range(0, feat_dim, LANES):
            part = cents_ref[pl.ds(start, LANES), pl.ds(lane, LANES)].astype(jnp.float32)
            total = total + part * part
        cent_sq_ref[:, pl.ds(start, LANES)] = jnp.sum(total.T, axis=0, keepdims=True)


def lanes(ref, row, count, tile, tiles):
    return ref.at[pl.ds(row * tiles + tile, count, stride=tiles), :]


def share_body(pos_ref, feats_ref, cents_ref, cent_sq_ref, vecs_ref, wt_hbm, kern_ref, part_ref, wt_ref, sems, *, step):
    gets = []
    for i in range(wt_hbm.shape[1] // step):
        cols = pl.ds(i * step, step)
        gets.append(pltpu.make_async_copy(wt_hbm.at[:, cols], wt_ref.at[:, cols], sems.at[i]))
        gets[-1].start()

    @pl.when(pos_ref[0] >= 0)
    def _():
        batch_total = feats_ref.shape[0]
        center_rows, feat_dim = cents_ref.shape
        classes = wt_ref.shape[0]
        eig_count = vecs_ref.shape[1] // 2
        tiles = part_ref.shape[0] // batch_total
        length = 1.5 / math.sqrt(feat_dim)
        feats = feats_ref[...]
        wide_feats = feats.astype(jnp.float32)
        row_sq = jnp.sum(wide_feats * wide_feats, axis=1, keepdims=True)
        for start in range(0, center_rows, step):
            cols = pl.ds(start, step)
            cross = dot32(feats, cents_ref[cols, :], NT)
            dist_sq = jnp.maximum(row_sq + cent_sq_ref[:, cols] - 2.0 * cross, 0.0)
            kern_ref[:, cols] = jnp.exp((1.4142 - jnp.sqrt(dist_sq)) / length).astype(jnp.bfloat16)
        coords = dot32(kern_ref[...], vecs_ref[...], NN)
        coords = coords[:, :eig_count] + coords[:, eig_count:]
        splits = list(range(0, classes, 256))
        totals = [None] * len(splits)
        for i, get in enumerate(gets):
            get.wait()
            for k in range(i * step, (i + 1) * step, 512):
                cols = pl.ds(k, 512)
                for n, row in enumerate(splits):
                    term = dot32(kern_ref[:, cols], wt_ref[pl.ds(row, min(256, classes - row)), cols], NT)
                    totals[n] = term if totals[n] is None else totals[n] + term
        total = jnp.concatenate(totals, axis=1)
        pad = jnp.zeros((batch_total, tiles * LANES - eig_count - classes), jnp.float32)
        part = jnp.concatenate([coords, total, pad], axis=1)
        for tile in range(tiles):
            for row in range(0, batch_total, 8):
                lanes(part_ref, row, 8, tile, tiles)[...] = part[row : row + 8, tile * LANES : (tile + 1) * LANES]


def settle_body(parts_ref, wanted_ref, both_ref, *, count):
    tiles = parts_ref.shape[0] // count
    for tile in range(tiles):
        total = jnp.sum(lanes(parts_ref, 0, count, tile, tiles)[...], axis=0, keepdims=True)
        total = total - wanted_ref[:, tile * LANES : (tile + 1) * LANES]
        lanes(both_ref, 0, count, tile, tiles)[...] = jnp.broadcast_to(total, (count, LANES))


def update_body(
    pos_ref, both_ref, scale_ref, kern_ref, vecs_ref, wt_ref, out_hbm, res_hbm,
    left_ref, factors_ref, new_ref, res_ref, sems, *, rate, sections, step, chunk
):
    fold = math.frexp(rate)[0] == 0.5
    classes = wt_ref.shape[0]
    batch_total = kern_ref.shape[0]
    eig_count = vecs_ref.shape[1] // 2
    first = eig_count // LANES
    tiles = both_ref.shape[0] // batch_total
    wide_count = batch_total // sections
    for tile in range(first, tiles):
        rows = lanes(both_ref, 0, batch_total, tile, tiles)[...].astype(jnp.bfloat16)
        if fold:
            rows = (rows.astype(jnp.float32) * rate).astype(jnp.bfloat16)
        turned = jnp.concatenate([rows, rows, rows, rows], axis=0).T
        left_ref[pl.ds((tile - first) * LANES, LANES), :] = turned
    coords = jnp.concatenate([lanes(both_ref, 0, batch_total, tile, tiles)[...] for tile in range(first)], axis=1)
    coords_hi, coords_lo = halves(coords * scale_ref[...])
    coords = jnp.concatenate([coords_hi, coords_lo], axis=0)
    coords = jnp.concatenate([coords, coords], axis=1)
    for start in range(0, wt_ref.shape[1], step):
        cols = pl.ds(start, step)
        drop = dot32(coords, vecs_ref[cols, :], NT)
        drop = drop[:batch_total] + drop[batch_total:]
        drop_hi, drop_lo = halves(-drop)
        factors_ref[:, cols] = jnp.concatenate([kern_ref[:, cols], drop_hi, drop_lo, jnp.zeros_like(drop_lo)], axis=0)
    puts = []
    for start in range(0, wt_ref.shape[1], step):
        cols = pl.ds(start, step)
        for row in range(0, classes, chunk):
            spot = (pl.ds(row, min(chunk, classes - row)), cols)
            grad = dot32(left_ref[spot[0], :], factors_ref[:, cols], NN)
            grad = grad if fold else rate * grad
            new_ref[spot] = (wt_ref[spot].astype(jnp.float32) - grad).astype(jnp.bfloat16)
            puts.append(pltpu.make_async_copy(new_ref.at[spot], out_hbm.at[spot], sems.at[len(puts)]))
            puts[-1].start()
        if start == 0:
            for s in range(sections):
                for tile in range(first, tiles):
                    width = min(LANES, classes - (tile - first) * LANES)
                    line = lanes(both_ref, s * wide_count + pos_ref[0], 1, tile, tiles)[...]
                    res_ref[pl.ds(s, 1), pl.ds((tile - first) * LANES, width)] = line[:, :width]
            puts.append(pltpu.make_async_copy(res_ref, res_hbm, sems.at[len(puts)]))
            puts[-1].start()
    for put in puts:
        put.wait()


def shards(train_feats, train_targets, batch_idx, centers, weights, nys_idx, eig_vecs, eig_scale):
    batch_rows = batch_idx.shape[0]
    center_rows, feat_dim = centers.shape
    classes = weights.shape[1]
    eig_count = eig_vecs.shape[1]
    wide_count = lax.axis_size("wide")
    sec_count = lax.axis_size("sec")
    wide_pos = lax.axis_index("wide")
    sec_pos = lax.axis_index("sec")
    batch_total = batch_rows * wide_count
    tiles = eig_count // LANES + pl.cdiv(classes, LANES)
    assert batch_rows == sec_count and eig_count % LANES == 0
    vmem = pl.BlockSpec(memory_space=pltpu.VMEM)
    smem = pl.BlockSpec(memory_space=pltpu.SMEM)
    hbm = pl.BlockSpec(memory_space=pltpu.HBM)

    params = pltpu.CompilerParams(vmem_limit_bytes=VMEM_GRANT)
    step = min(512, center_rows // 4)
    chunk = 512

    copies = pl.pallas_call(
        gather_body,
        out_shape=jax.ShapeDtypeStruct((wide_count, batch_rows, feat_dim), jnp.bfloat16),
        in_specs=[smem, hbm, hbm],
        out_specs=vmem,
        scratch_shapes=[
            pltpu.SMEM((batch_rows,), jnp.int32),
            pltpu.VMEM(train_feats.shape, train_feats.dtype),
            pltpu.SemaphoreType.DMA((2,)),
        ],
        compiler_params=params,
        name="gather",
    )(wide_pos[None], in_hbm(batch_idx), in_hbm(train_feats))
    piece = lax.all_to_all(copies, "wide", 0, 0, tiled=False)
    piece = jnp.transpose(piece, (1, 0, 2)).reshape(batch_total, feat_dim)

    turned_weights = in_hbm(weights.T)
    staged_centers, cent_sq, vecs, wanted = pl.pallas_call(
        functools.partial(stage_body, wide_count=wide_count),
        out_shape=(
            jax.ShapeDtypeStruct(centers.shape, centers.dtype),
            jax.ShapeDtypeStruct((1, center_rows), jnp.float32),
            jax.ShapeDtypeStruct((center_rows, 2 * eig_count), jnp.bfloat16),
            jax.ShapeDtypeStruct((1, tiles * LANES), jnp.float32),
        ),
        in_specs=[smem] + [hbm] * 5,
        out_specs=(vmem,) * 4,
        scratch_shapes=[
            pltpu.VMEM((1, nys_idx.shape[0]), jnp.int32),
            pltpu.VMEM(eig_vecs.shape, jnp.float32),
            pltpu.SMEM((batch_rows,), jnp.int32),
            pltpu.VMEM(train_targets.shape, jnp.float32),
            pltpu.SemaphoreType.DMA((5,)),
        ],
        compiler_params=params,
        cost_estimate=pl.CostEstimate(flops=1 << 31, bytes_accessed=16 << 20, transcendentals=0),
        name="stage",
    )(
        (sec_pos * wide_count + wide_pos)[None],
        in_hbm(nys_idx[None, :]),
        in_hbm(eig_vecs),
        in_hbm(batch_idx),
        in_hbm(train_targets),
        in_hbm(centers),
    )

    slab_count = center_rows // step
    kern, part, kept = pl.pallas_call(
        functools.partial(share_body, step=step),
        out_shape=(
            jax.ShapeDtypeStruct((batch_total, center_rows), jnp.bfloat16),
            jax.ShapeDtypeStruct((batch_total * tiles, LANES), jnp.float32),
            jax.ShapeDtypeStruct((classes, center_rows), jnp.bfloat16),
        ),
        in_specs=[smem] + [vmem] * 4 + [hbm],
        out_specs=(vmem, vmem, vmem),
        scratch_shapes=[pltpu.SemaphoreType.DMA((slab_count,))],
        compiler_params=params,
        name="share",
    )(wide_pos[None], piece, staged_centers, cent_sq, vecs, turned_weights)

    parts = lax.all_to_all(part.reshape(batch_total, 1, tiles * LANES), ("sec", "wide"), 0, 0, tiled=False)
    both = pl.pallas_call(
        functools.partial(settle_body, count=batch_total),
        out_shape=jax.ShapeDtypeStruct((batch_total * tiles, LANES), jnp.float32),
        in_specs=[vmem, vmem],
        out_specs=vmem,
        compiler_params=params,
        name="settle",
    )(parts.reshape(batch_total * tiles, LANES), wanted)
    both = lax.all_to_all(both.reshape(batch_total, 1, tiles * LANES), ("sec", "wide"), 0, 0, tiled=False)
    both = both.reshape(batch_total * tiles, LANES)

    new_turned, residual = pl.pallas_call(
        functools.partial(update_body, rate=16.0 / batch_total, sections=sec_count, step=step, chunk=chunk),
        out_shape=(
            jax.ShapeDtypeStruct((classes, center_rows), jnp.bfloat16),
            jax.ShapeDtypeStruct((batch_rows, classes), jnp.float32),
        ),
        in_specs=[smem] + [vmem] * 5,
        out_specs=(hbm, hbm),
        scratch_shapes=[
            pltpu.VMEM((pl.cdiv(classes, LANES) * LANES, 4 * batch_total), jnp.bfloat16),
            pltpu.VMEM((4 * batch_total, center_rows), jnp.bfloat16),
            pltpu.VMEM((classes, center_rows), jnp.bfloat16),
            pltpu.VMEM((batch_rows, classes), jnp.float32),
            pltpu.SemaphoreType.DMA((1 + slab_count * pl.cdiv(classes, chunk),)),
        ],
        compiler_params=params,
        name="update",
    )(wide_pos[None], both, eig_scale[None, :], kern, vecs, kept)
    return (new_turned.T, residual)


def solution(mesh):
    return jax.shard_map(
        shards,
        mesh=mesh,
        in_specs=(
            P("wide", None),
            P("wide", None),
            P("wide"),
            P(("sec", "wide"), None),
            P(("sec", "wide"), None),
            P("wide"),
            P("wide", None),
            P(),
        ),
        out_specs=(P(("sec", "wide"), None), P("wide", None)),
        check_vma=False,
    )
```

```python
import functools
import math

import jax
import jax.numpy as jnp
from jax import lax
from jax.experimental import pallas as pl
from jax.experimental.pallas import tpu as pltpu
from jax.sharding import PartitionSpec as P

LANES = 128
LINES = 4
VMEM_GRANT = 16 << 20
NT = (((1,), (1,)), ((), ()))
NN = (((1,), (0,)), ((), ()))


def dot32(a, b, dims):
    return lax.dot_general(a, b, dims, preferred_element_type=jnp.float32)


def halves(x):
    top = x.astype(jnp.bfloat16)
    return top, (x - top.astype(jnp.float32)).astype(jnp.bfloat16)


def in_hbm(x):
    return pltpu.with_memory_space_constraint(x, pltpu.HBM)


def gather_body(pos_ref, idx_hbm, rows_hbm, out_ref, idx_ref, rows_ref, sems):
    get_idx = pltpu.make_async_copy(idx_hbm, idx_ref, sems.at[0])
    get_rows = pltpu.make_async_copy(rows_hbm, rows_ref, sems.at[1])
    get_idx.start()
    get_rows.start()
    get_idx.wait()
    pool_rows = rows_ref.shape[0]
    copies, batch_rows = out_ref.shape[:2]
    shape = (batch_rows, pool_rows)
    row = lax.broadcasted_iota(jnp.int32, shape, 0)
    wanted = jnp.zeros(shape, jnp.int32)
    for j in range(batch_rows):
        wanted = jnp.where(row == j, idx_ref[j] - pos_ref[0] * pool_rows, wanted)
    picked = (lax.broadcasted_iota(jnp.int32, shape, 1) == wanted).astype(jnp.bfloat16)
    get_rows.wait()
    rows = dot32(picked, rows_ref[...], NN).astype(jnp.bfloat16)
    for w in range(copies):
        out_ref[w] = rows


def stage_body(
    pos_ref, nys_hbm, eig_hbm, idx_hbm, targets_hbm, cents_hbm, cents_ref, cent_sq_ref, vecs_ref, wanted_ref,
    nys_ref, eig_ref, idx_ref, targets_ref, sems, *, wide_count
):
    pairs = (
        (nys_hbm, nys_ref), (eig_hbm, eig_ref), (idx_hbm, idx_ref), (targets_hbm, targets_ref), (cents_hbm, cents_ref)
    )
    gets = [pltpu.make_async_copy(src, dst, sems.at[i]) for i, (src, dst) in enumerate(pairs)]
    for get in gets:
        get.start()
    gets[0].wait()
    gets[1].wait()
    center_rows, feat_dim = cents_ref.shape
    nys_count, eig_count = eig_ref.shape
    eig_both = jnp.concatenate(halves(eig_ref[...]), axis=1)
    place = nys_ref[...] - pos_ref[0] * center_rows
    for start in range(0, center_rows, LANES):
        rows = pl.ds(start, LANES)
        at = lax.broadcasted_iota(jnp.int32, (LANES, nys_count), 0) + start
        moved = dot32((at == place).astype(jnp.bfloat16), eig_both, NN)
        vec_hi, vec_lo = halves(moved[:, :eig_count] + moved[:, eig_count:])
        vecs_ref[rows, :eig_count] = vec_hi
        vecs_ref[rows, eig_count:] = vec_lo
    gets[2].wait()
    gets[3].wait()
    pool_rows, classes = targets_ref.shape
    row = idx_ref[pos_ref[0] // wide_count] - pos_ref[0] % wide_count * pool_rows
    wanted_ref[...] = jnp.zeros_like(wanted_ref)
    wanted_ref[:, pl.ds(eig_count, classes)] = targets_ref[pl.ds(row, 1), :]
    gets[4].wait()
    for start in range(0, center_rows, LANES):
        total = jnp.zeros((LANES, LANES), jnp.float32)
        for lane in range(0, feat_dim, LANES):
            part = cents_ref[pl.ds(start, LANES), pl.ds(lane, LANES)].astype(jnp.float32)
            total = total + part * part
        cent_sq_ref[:, pl.ds(start, LANES)] = jnp.sum(total.T, axis=0, keepdims=True)


def lanes(ref, row, count, tile, tiles):
    return ref.at[pl.ds(row * tiles + tile, count, stride=tiles), :]


def share_body(pos_ref, feats_ref, cents_ref, cent_sq_ref, vecs_ref, wt_hbm, kern_ref, part_ref, wt_ref, sems, *, step):
    gets = []
    for i in range(wt_hbm.shape[1] // step):
        cols = pl.ds(i * step, step)
        gets.append(pltpu.make_async_copy(wt_hbm.at[:, cols], wt_ref.at[:, cols], sems.at[i]))
        gets[-1].start()

    @pl.when(pos_ref[0] >= 0)
    def _():
        batch_total = feats_ref.shape[0]
        center_rows, feat_dim = cents_ref.shape
        classes = wt_ref.shape[0]
        eig_count = vecs_ref.shape[1] // 2
        tiles = part_ref.shape[0] // batch_total
        length = 1.5 / math.sqrt(feat_dim)
        feats = feats_ref[...]
        wide_feats = feats.astype(jnp.float32)
        row_sq = jnp.sum(wide_feats * wide_feats, axis=1, keepdims=True)
        for start in range(0, center_rows, step):
            cols = pl.ds(start, step)
            cross = dot32(feats, cents_ref[cols, :], NT)
            dist_sq = jnp.maximum(row_sq + cent_sq_ref[:, cols] - 2.0 * cross, 0.0)
            kern_ref[:, cols] = jnp.exp((1.4142 - jnp.sqrt(dist_sq)) / length).astype(jnp.bfloat16)
        coords = dot32(kern_ref[...], vecs_ref[...], NN)
        coords = coords[:, :eig_count] + coords[:, eig_count:]
        splits = list(range(0, classes, 256))
        totals = [None] * len(splits)
        for i, get in enumerate(gets):
            get.wait()
            for k in range(i * step, (i + 1) * step, 512):
                cols = pl.ds(k, 512)
                for n, row in enumerate(splits):
                    term = dot32(kern_ref[:, cols], wt_ref[pl.ds(row, min(256, classes - row)), cols], NT)
                    totals[n] = term if totals[n] is None else totals[n] + term
        total = jnp.concatenate(totals, axis=1)
        pad = jnp.zeros((batch_total, tiles * LANES - eig_count - classes), jnp.float32)
        part = jnp.concatenate([coords, total, pad], axis=1)
        for tile in range(tiles):
            for row in range(0, batch_total, 8):
                lanes(part_ref, row, 8, tile, tiles)[...] = part[row : row + 8, tile * LANES : (tile + 1) * LANES]


def settle_body(parts_ref, wanted_ref, both_ref, *, first):
    count, lines, width = both_ref.shape
    tiles = parts_ref.shape[0] // count
    pieces = []
    coords = []
    for tile in range(tiles):
        total = jnp.sum(lanes(parts_ref, 0, count, tile, tiles)[...], axis=0, keepdims=True)
        total = total - wanted_ref[:, tile * LANES : (tile + 1) * LANES]
        (coords if tile < first else pieces).append(total)
    for _ in range(3):
        pieces += [total.astype(jnp.bfloat16).astype(jnp.float32) for total in coords]
        coords = [total - piece for total, piece in zip(coords, pieces[-first:])]
    blocks = width // LANES
    pieces += [jnp.zeros_like(pieces[0])] * (lines * blocks - len(pieces))
    out = jnp.zeros((lines, width), jnp.float32)
    for line in range(lines):
        whole = jnp.concatenate(pieces[line * blocks : (line + 1) * blocks], axis=1)
        out = jnp.where(lax.broadcasted_iota(jnp.int32, out.shape, 0) == line, whole, out)
    out = out.astype(jnp.bfloat16)
    for device in range(count):
        both_ref[device] = out


def update_body(
    pos_ref, both_ref, scale_ref, kern_ref, vecs_ref, wt_ref, out_hbm, res_hbm,
    flat_ref, left_ref, factors_ref, new_ref, res_ref, sems, *, rate, sections, step, chunk
):
    fold = math.frexp(rate)[0] == 0.5
    classes = wt_ref.shape[0]
    batch_total, lines, width = both_ref.shape
    wide_count = batch_total // sections
    blocks = width // LANES
    eig_count = vecs_ref.shape[1] // 2
    first = eig_count // LANES
    res_tiles = pl.cdiv(classes, LANES)
    flat = both_ref[...].astype(jnp.float32).reshape(batch_total * lines, width)
    for block in range(blocks):
        flat_ref[pl.ds(block * batch_total * lines, batch_total * lines), :] = flat[:, block * LANES : (block + 1) * LANES]

    def piece(tile, row, count):
        line, block = divmod(tile, blocks)
        return flat_ref[pl.ds((block * batch_total + row) * lines + line, count, stride=lines), :]

    for tile in range(res_tiles):
        rows = piece(tile, 0, batch_total)
        rows = (rows * rate if fold else rows).astype(jnp.bfloat16)
        left_ref[pl.ds(tile * LANES, LANES), :] = jnp.concatenate([rows, rows, rows, rows], axis=0).T
    parts = [jnp.concatenate([piece(res_tiles + i * first + tile, 0, batch_total) for tile in range(first)], axis=1) for i in range(3)]
    coords_hi, coords_lo = halves((parts[0] + parts[1] + parts[2]) * scale_ref[...])
    coords = jnp.concatenate([coords_hi, coords_lo], axis=0)
    coords = jnp.concatenate([coords, coords], axis=1)
    for start in range(0, wt_ref.shape[1], step):
        cols = pl.ds(start, step)
        drop = dot32(coords, vecs_ref[cols, :], NT)
        drop = drop[:batch_total] + drop[batch_total:]
        drop_hi, drop_lo = halves(-drop)
        factors_ref[:, cols] = jnp.concatenate([kern_ref[:, cols], drop_hi, drop_lo, jnp.zeros_like(drop_lo)], axis=0)
    puts = []
    for start in range(0, wt_ref.shape[1], step):
        cols = pl.ds(start, step)
        for row in range(0, classes, chunk):
            spot = (pl.ds(row, min(chunk, classes - row)), cols)
            grad = dot32(left_ref[spot[0], :], factors_ref[:, cols], NN)
            grad = grad if fold else rate * grad
            new_ref[spot] = (wt_ref[spot].astype(jnp.float32) - grad).astype(jnp.bfloat16)
            puts.append(pltpu.make_async_copy(new_ref.at[spot], out_hbm.at[spot], sems.at[len(puts)]))
            puts[-1].start()
        if start == 0:
            for s in range(sections):
                for tile in range(res_tiles):
                    size = min(LANES, classes - tile * LANES)
                    line = piece(tile, s * wide_count + pos_ref[0], 1)
                    res_ref[pl.ds(s, 1), pl.ds(tile * LANES, size)] = line[:, :size]
            puts.append(pltpu.make_async_copy(res_ref, res_hbm, sems.at[len(puts)]))
            puts[-1].start()
    for put in puts:
        put.wait()


def shards(train_feats, train_targets, batch_idx, centers, weights, nys_idx, eig_vecs, eig_scale):
    batch_rows = batch_idx.shape[0]
    center_rows, feat_dim = centers.shape
    classes = weights.shape[1]
    eig_count = eig_vecs.shape[1]
    wide_count = lax.axis_size("wide")
    sec_count = lax.axis_size("sec")
    wide_pos = lax.axis_index("wide")
    sec_pos = lax.axis_index("sec")
    batch_total = batch_rows * wide_count
    tiles = eig_count // LANES + pl.cdiv(classes, LANES)
    assert batch_rows == sec_count and eig_count % LANES == 0
    vmem = pl.BlockSpec(memory_space=pltpu.VMEM)
    smem = pl.BlockSpec(memory_space=pltpu.SMEM)
    hbm = pl.BlockSpec(memory_space=pltpu.HBM)

    params = pltpu.CompilerParams(vmem_limit_bytes=VMEM_GRANT)
    step = min(512, center_rows // 4)
    chunk = 512

    copies = pl.pallas_call(
        gather_body,
        out_shape=jax.ShapeDtypeStruct((wide_count, batch_rows, feat_dim), jnp.bfloat16),
        in_specs=[smem, hbm, hbm],
        out_specs=vmem,
        scratch_shapes=[
            pltpu.SMEM((batch_rows,), jnp.int32),
            pltpu.VMEM(train_feats.shape, train_feats.dtype),
            pltpu.SemaphoreType.DMA((2,)),
        ],
        compiler_params=params,
        name="gather",
    )(wide_pos[None], in_hbm(batch_idx), in_hbm(train_feats))
    piece = lax.all_to_all(copies, "wide", 0, 0, tiled=False)
    piece = jnp.transpose(piece, (1, 0, 2)).reshape(batch_total, feat_dim)

    turned_weights = in_hbm(weights.T)
    staged_centers, cent_sq, vecs, wanted = pl.pallas_call(
        functools.partial(stage_body, wide_count=wide_count),
        out_shape=(
            jax.ShapeDtypeStruct(centers.shape, centers.dtype),
            jax.ShapeDtypeStruct((1, center_rows), jnp.float32),
            jax.ShapeDtypeStruct((center_rows, 2 * eig_count), jnp.bfloat16),
            jax.ShapeDtypeStruct((1, tiles * LANES), jnp.float32),
        ),
        in_specs=[smem] + [hbm] * 5,
        out_specs=(vmem,) * 4,
        scratch_shapes=[
            pltpu.VMEM((1, nys_idx.shape[0]), jnp.int32),
            pltpu.VMEM(eig_vecs.shape, jnp.float32),
            pltpu.SMEM((batch_rows,), jnp.int32),
            pltpu.VMEM(train_targets.shape, jnp.float32),
            pltpu.SemaphoreType.DMA((5,)),
        ],
        compiler_params=params,
        cost_estimate=pl.CostEstimate(flops=1 << 31, bytes_accessed=16 << 20, transcendentals=0),
        name="stage",
    )(
        (sec_pos * wide_count + wide_pos)[None],
        in_hbm(nys_idx[None, :]),
        in_hbm(eig_vecs),
        in_hbm(batch_idx),
        in_hbm(train_targets),
        in_hbm(centers),
    )

    slab_count = center_rows // step
    kern, part, kept = pl.pallas_call(
        functools.partial(share_body, step=step),
        out_shape=(
            jax.ShapeDtypeStruct((batch_total, center_rows), jnp.bfloat16),
            jax.ShapeDtypeStruct((batch_total * tiles, LANES), jnp.float32),
            jax.ShapeDtypeStruct((classes, center_rows), jnp.bfloat16),
        ),
        in_specs=[smem] + [vmem] * 4 + [hbm],
        out_specs=(vmem, vmem, vmem),
        scratch_shapes=[pltpu.SemaphoreType.DMA((slab_count,))],
        compiler_params=params,
        name="share",
    )(wide_pos[None], piece, staged_centers, cent_sq, vecs, turned_weights)

    parts = lax.all_to_all(part.reshape(batch_total, 1, tiles * LANES), ("sec", "wide"), 0, 0, tiled=False)
    first = eig_count // LANES
    blocks = pl.cdiv(tiles + 2 * first, LINES)
    both = pl.pallas_call(
        functools.partial(settle_body, first=first),
        out_shape=jax.ShapeDtypeStruct((batch_total, LINES, blocks * LANES), jnp.bfloat16),
        in_specs=[vmem, vmem],
        out_specs=vmem,
        compiler_params=params,
        name="settle",
    )(parts.reshape(batch_total * tiles, LANES), wanted)
    both = lax.all_to_all(both, ("sec", "wide"), 0, 0, tiled=False)

    new_turned, residual = pl.pallas_call(
        functools.partial(update_body, rate=16.0 / batch_total, sections=sec_count, step=step, chunk=chunk),
        out_shape=(
            jax.ShapeDtypeStruct((classes, center_rows), jnp.bfloat16),
            jax.ShapeDtypeStruct((batch_rows, classes), jnp.float32),
        ),
        in_specs=[smem] + [vmem] * 5,
        out_specs=(hbm, hbm),
        scratch_shapes=[
            pltpu.VMEM((blocks * batch_total * LINES, LANES), jnp.float32),
            pltpu.VMEM((pl.cdiv(classes, LANES) * LANES, 4 * batch_total), jnp.bfloat16),
            pltpu.VMEM((4 * batch_total, center_rows), jnp.bfloat16),
            pltpu.VMEM((classes, center_rows), jnp.bfloat16),
            pltpu.VMEM((batch_rows, classes), jnp.float32),
            pltpu.SemaphoreType.DMA((1 + slab_count * pl.cdiv(classes, chunk),)),
        ],
        compiler_params=params,
        name="update",
    )(wide_pos[None], both, eig_scale[None, :], kern, vecs, kept)
    return (new_turned.T, residual)


def solution(mesh):
    return jax.shard_map(
        shards,
        mesh=mesh,
        in_specs=(
            P("wide", None),
            P("wide", None),
            P("wide"),
            P(("sec", "wide"), None),
            P(("sec", "wide"), None),
            P("wide"),
            P("wide", None),
            P(),
        ),
        out_specs=(P(("sec", "wide"), None), P("wide", None)),
        check_vma=False,
    )
```

```python
import functools
import math

import jax
import jax.numpy as jnp
from jax import lax
from jax.experimental import pallas as pl
from jax.experimental.pallas import tpu as pltpu
from jax.sharding import PartitionSpec as P

LANES = 128
LINES = 4
VMEM_GRANT = 16 << 20
NT = (((1,), (1,)), ((), ()))
NN = (((1,), (0,)), ((), ()))


def dot32(a, b, dims):
    return lax.dot_general(a, b, dims, preferred_element_type=jnp.float32)


def halves(x):
    top = x.astype(jnp.bfloat16)
    return top, (x - top.astype(jnp.float32)).astype(jnp.bfloat16)


def in_hbm(x):
    return pltpu.with_memory_space_constraint(x, pltpu.HBM)


def gather_body(pos_ref, idx_hbm, rows_hbm, out_ref, idx_ref, rows_ref, sems):
    get_idx = pltpu.make_async_copy(idx_hbm, idx_ref, sems.at[0])
    get_rows = pltpu.make_async_copy(rows_hbm, rows_ref, sems.at[1])
    get_idx.start()
    get_rows.start()
    get_idx.wait()
    pool_rows = rows_ref.shape[0]
    copies, batch_rows = out_ref.shape[:2]
    shape = (batch_rows, pool_rows)
    row = lax.broadcasted_iota(jnp.int32, shape, 0)
    wanted = jnp.zeros(shape, jnp.int32)
    for j in range(batch_rows):
        wanted = jnp.where(row == j, idx_ref[j] - pos_ref[0] * pool_rows, wanted)
    picked = (lax.broadcasted_iota(jnp.int32, shape, 1) == wanted).astype(jnp.bfloat16)
    get_rows.wait()
    rows = dot32(picked, rows_ref[...], NN).astype(jnp.bfloat16)
    for w in range(copies):
        out_ref[w] = rows


def stage_body(
    pos_ref, nys_hbm, eig_hbm, idx_hbm, targets_hbm, cents_hbm, cents_ref, cent_sq_ref, vecs_ref, wanted_ref,
    nys_ref, eig_ref, idx_ref, targets_ref, sems, *, wide_count
):
    pairs = (
        (nys_hbm, nys_ref), (eig_hbm, eig_ref), (idx_hbm, idx_ref), (targets_hbm, targets_ref), (cents_hbm, cents_ref)
    )
    gets = [pltpu.make_async_copy(src, dst, sems.at[i]) for i, (src, dst) in enumerate(pairs)]
    for get in gets:
        get.start()
    gets[0].wait()
    gets[1].wait()
    center_rows, feat_dim = cents_ref.shape
    nys_count, eig_count = eig_ref.shape
    eig_both = jnp.concatenate(halves(eig_ref[...]), axis=1)
    place = nys_ref[...] - pos_ref[0] * center_rows
    for start in range(0, center_rows, LANES):
        rows = pl.ds(start, LANES)
        at = lax.broadcasted_iota(jnp.int32, (LANES, nys_count), 0) + start
        moved = dot32((at == place).astype(jnp.bfloat16), eig_both, NN)
        vec_hi, vec_lo = halves(moved[:, :eig_count] + moved[:, eig_count:])
        vecs_ref[rows, :eig_count] = vec_hi
        vecs_ref[rows, eig_count:] = vec_lo
    gets[2].wait()
    gets[3].wait()
    pool_rows, classes = targets_ref.shape
    row = idx_ref[pos_ref[0] // wide_count] - pos_ref[0] % wide_count * pool_rows
    wanted_ref[...] = jnp.zeros_like(wanted_ref)
    wanted_ref[:, pl.ds(eig_count, classes)] = targets_ref[pl.ds(row, 1), :]
    gets[4].wait()
    for start in range(0, center_rows, LANES):
        total = jnp.zeros((LANES, LANES), jnp.float32)
        for lane in range(0, feat_dim, LANES):
            part = cents_ref[pl.ds(start, LANES), pl.ds(lane, LANES)].astype(jnp.float32)
            total = total + part * part
        cent_sq_ref[:, pl.ds(start, LANES)] = jnp.sum(total.T, axis=0, keepdims=True)


def lanes(ref, row, count, tile, tiles):
    return ref.at[pl.ds(row * tiles + tile, count, stride=tiles), :]


def share_body(pos_ref, feats_ref, cents_ref, cent_sq_ref, vecs_ref, wt_hbm, kern_ref, part_ref, wt_ref, sems, *, step):
    gets = []
    for i in range(wt_hbm.shape[1] // step):
        cols = pl.ds(i * step, step)
        gets.append(pltpu.make_async_copy(wt_hbm.at[:, cols], wt_ref.at[:, cols], sems.at[i]))
        gets[-1].start()

    @pl.when(pos_ref[0] >= 0)
    def _():
        batch_total = feats_ref.shape[0]
        center_rows, feat_dim = cents_ref.shape
        classes = wt_ref.shape[0]
        eig_count = vecs_ref.shape[1] // 2
        tiles = part_ref.shape[0] // batch_total
        length = 1.5 / math.sqrt(feat_dim)
        feats = feats_ref[...]
        wide_feats = feats.astype(jnp.float32)
        row_sq = jnp.sum(wide_feats * wide_feats, axis=1, keepdims=True)
        for start in range(0, center_rows, step):
            cols = pl.ds(start, step)
            cross = dot32(feats, cents_ref[cols, :], NT)
            dist_sq = jnp.maximum(row_sq + cent_sq_ref[:, cols] - 2.0 * cross, 0.0)
            kern_ref[:, cols] = jnp.exp((1.4142 - jnp.sqrt(dist_sq)) / length).astype(jnp.bfloat16)
        coords = dot32(kern_ref[...], vecs_ref[...], NN)
        coords = coords[:, :eig_count] + coords[:, eig_count:]
        splits = list(range(0, classes, 256))
        totals = [None] * len(splits)
        for i, get in enumerate(gets):
            get.wait()
            for k in range(i * step, (i + 1) * step, 512):
                cols = pl.ds(k, 512)
                for n, row in enumerate(splits):
                    term = dot32(kern_ref[:, cols], wt_ref[pl.ds(row, min(256, classes - row)), cols], NT)
                    totals[n] = term if totals[n] is None else totals[n] + term
        total = jnp.concatenate(totals, axis=1)
        pad = jnp.zeros((batch_total, tiles * LANES - eig_count - classes), jnp.float32)
        part = jnp.concatenate([coords, total, pad], axis=1)
        for tile in range(tiles):
            for row in range(0, batch_total, 8):
                lanes(part_ref, row, 8, tile, tiles)[...] = part[row : row + 8, tile * LANES : (tile + 1) * LANES]


def settle_body(parts_ref, wanted_ref, both_ref, *, first):
    count, lines, width = both_ref.shape
    tiles = parts_ref.shape[0] // count
    pieces = []
    coords = []
    for tile in range(tiles):
        total = jnp.sum(lanes(parts_ref, 0, count, tile, tiles)[...], axis=0, keepdims=True)
        total = total - wanted_ref[:, tile * LANES : (tile + 1) * LANES]
        (coords if tile < first else pieces).append(total)
    for _ in range(3):
        pieces += [total.astype(jnp.bfloat16).astype(jnp.float32) for total in coords]
        coords = [total - piece for total, piece in zip(coords, pieces[-first:])]
    blocks = width // LANES
    pieces += [jnp.zeros_like(pieces[0])] * (lines * blocks - len(pieces))
    out = jnp.zeros((lines, width), jnp.float32)
    for line in range(lines):
        whole = jnp.concatenate(pieces[line * blocks : (line + 1) * blocks], axis=1)
        out = jnp.where(lax.broadcasted_iota(jnp.int32, out.shape, 0) == line, whole, out)
    out = out.astype(jnp.bfloat16)
    for device in range(count):
        both_ref[device] = out


def update_body(
    pos_ref, both_ref, scale_ref, kern_ref, vecs_ref, wt_ref, out_hbm, res_hbm,
    flat_ref, left_ref, factors_ref, new_ref, res_ref, sems, *, rate, sections, step, chunk
):
    fold = math.frexp(rate)[0] == 0.5
    classes = wt_ref.shape[0]
    batch_total, lines, width = both_ref.shape
    wide_count = batch_total // sections
    blocks = width // LANES
    eig_count = vecs_ref.shape[1] // 2
    first = eig_count // LANES
    res_tiles = pl.cdiv(classes, LANES)
    flat = both_ref[...].astype(jnp.float32).reshape(batch_total * lines, width)
    for block in range(blocks):
        flat_ref[pl.ds(block * batch_total * lines, batch_total * lines), :] = flat[:, block * LANES : (block + 1) * LANES]

    def piece(tile, row, count):
        line, block = divmod(tile, blocks)
        return flat_ref[pl.ds((block * batch_total + row) * lines + line, count, stride=lines), :]

    for tile in range(res_tiles):
        rows = piece(tile, 0, batch_total)
        rows = (rows * rate if fold else rows).astype(jnp.bfloat16)
        left_ref[pl.ds(tile * LANES, LANES), :] = jnp.concatenate([rows, rows, rows, rows], axis=0).T
    parts = [jnp.concatenate([piece(res_tiles + i * first + tile, 0, batch_total) for tile in range(first)], axis=1) for i in range(3)]
    coords_hi, coords_lo = halves((parts[0] + parts[1] + parts[2]) * scale_ref[...])
    coords = jnp.concatenate([coords_hi, coords_lo], axis=0)
    coords = jnp.concatenate([coords, coords], axis=1)
    def make(start):
        cols = pl.ds(start, step)
        drop = dot32(coords, vecs_ref[cols, :], NT)
        drop = drop[:batch_total] + drop[batch_total:]
        drop_hi, drop_lo = halves(-drop)
        factors_ref[:, cols] = jnp.concatenate([kern_ref[:, cols], drop_hi, drop_lo, jnp.zeros_like(drop_lo)], axis=0)

    make(0)
    puts = []
    for start in range(0, wt_ref.shape[1], step):
        cols = pl.ds(start, step)
        if start + step < wt_ref.shape[1]:
            make(start + step)
        for row in range(0, classes, chunk):
            spot = (pl.ds(row, min(chunk, classes - row)), cols)
            grad = dot32(left_ref[spot[0], :], factors_ref[:, cols], NN)
            grad = grad if fold else rate * grad
            new_ref[spot] = (wt_ref[spot].astype(jnp.float32) - grad).astype(jnp.bfloat16)
            puts.append(pltpu.make_async_copy(new_ref.at[spot], out_hbm.at[spot], sems.at[len(puts)]))
            puts[-1].start()
        if start == 0:
            for s in range(sections):
                for tile in range(res_tiles):
                    size = min(LANES, classes - tile * LANES)
                    line = piece(tile, s * wide_count + pos_ref[0], 1)
                    res_ref[pl.ds(s, 1), pl.ds(tile * LANES, size)] = line[:, :size]
            puts.append(pltpu.make_async_copy(res_ref, res_hbm, sems.at[len(puts)]))
            puts[-1].start()
    for put in puts:
        put.wait()


def shards(train_feats, train_targets, batch_idx, centers, weights, nys_idx, eig_vecs, eig_scale):
    batch_rows = batch_idx.shape[0]
    center_rows, feat_dim = centers.shape
    classes = weights.shape[1]
    eig_count = eig_vecs.shape[1]
    wide_count = lax.axis_size("wide")
    sec_count = lax.axis_size("sec")
    wide_pos = lax.axis_index("wide")
    sec_pos = lax.axis_index("sec")
    batch_total = batch_rows * wide_count
    tiles = eig_count // LANES + pl.cdiv(classes, LANES)
    assert batch_rows == sec_count and eig_count % LANES == 0
    vmem = pl.BlockSpec(memory_space=pltpu.VMEM)
    smem = pl.BlockSpec(memory_space=pltpu.SMEM)
    hbm = pl.BlockSpec(memory_space=pltpu.HBM)

    params = pltpu.CompilerParams(vmem_limit_bytes=VMEM_GRANT)
    step = min(512, center_rows // 4)
    chunk = 512

    copies = pl.pallas_call(
        gather_body,
        out_shape=jax.ShapeDtypeStruct((wide_count, batch_rows, feat_dim), jnp.bfloat16),
        in_specs=[smem, hbm, hbm],
        out_specs=vmem,
        scratch_shapes=[
            pltpu.SMEM((batch_rows,), jnp.int32),
            pltpu.VMEM(train_feats.shape, train_feats.dtype),
            pltpu.SemaphoreType.DMA((2,)),
        ],
        compiler_params=params,
        name="gather",
    )(wide_pos[None], in_hbm(batch_idx), in_hbm(train_feats))
    piece = lax.all_to_all(copies, "wide", 0, 0, tiled=False)
    piece = jnp.transpose(piece, (1, 0, 2)).reshape(batch_total, feat_dim)

    turned_weights = in_hbm(weights.T)
    staged_centers, cent_sq, vecs, wanted = pl.pallas_call(
        functools.partial(stage_body, wide_count=wide_count),
        out_shape=(
            jax.ShapeDtypeStruct(centers.shape, centers.dtype),
            jax.ShapeDtypeStruct((1, center_rows), jnp.float32),
            jax.ShapeDtypeStruct((center_rows, 2 * eig_count), jnp.bfloat16),
            jax.ShapeDtypeStruct((1, tiles * LANES), jnp.float32),
        ),
        in_specs=[smem] + [hbm] * 5,
        out_specs=(vmem,) * 4,
        scratch_shapes=[
            pltpu.VMEM((1, nys_idx.shape[0]), jnp.int32),
            pltpu.VMEM(eig_vecs.shape, jnp.float32),
            pltpu.SMEM((batch_rows,), jnp.int32),
            pltpu.VMEM(train_targets.shape, jnp.float32),
            pltpu.SemaphoreType.DMA((5,)),
        ],
        compiler_params=params,
        cost_estimate=pl.CostEstimate(flops=1 << 31, bytes_accessed=16 << 20, transcendentals=0),
        name="stage",
    )(
        (sec_pos * wide_count + wide_pos)[None],
        in_hbm(nys_idx[None, :]),
        in_hbm(eig_vecs),
        in_hbm(batch_idx),
        in_hbm(train_targets),
        in_hbm(centers),
    )

    slab_count = center_rows // step
    kern, part, kept = pl.pallas_call(
        functools.partial(share_body, step=step),
        out_shape=(
            jax.ShapeDtypeStruct((batch_total, center_rows), jnp.bfloat16),
            jax.ShapeDtypeStruct((batch_total * tiles, LANES), jnp.float32),
            jax.ShapeDtypeStruct((classes, center_rows), jnp.bfloat16),
        ),
        in_specs=[smem] + [vmem] * 4 + [hbm],
        out_specs=(vmem, vmem, vmem),
        scratch_shapes=[pltpu.SemaphoreType.DMA((slab_count,))],
        compiler_params=params,
        name="share",
    )(wide_pos[None], piece, staged_centers, cent_sq, vecs, turned_weights)

    parts = lax.all_to_all(part.reshape(batch_total, 1, tiles * LANES), ("sec", "wide"), 0, 0, tiled=False)
    first = eig_count // LANES
    blocks = pl.cdiv(tiles + 2 * first, LINES)
    both = pl.pallas_call(
        functools.partial(settle_body, first=first),
        out_shape=jax.ShapeDtypeStruct((batch_total, LINES, blocks * LANES), jnp.bfloat16),
        in_specs=[vmem, vmem],
        out_specs=vmem,
        compiler_params=params,
        name="settle",
    )(parts.reshape(batch_total * tiles, LANES), wanted)
    both = lax.all_to_all(both, ("sec", "wide"), 0, 0, tiled=False)

    new_turned, residual = pl.pallas_call(
        functools.partial(update_body, rate=16.0 / batch_total, sections=sec_count, step=step, chunk=chunk),
        out_shape=(
            jax.ShapeDtypeStruct((classes, center_rows), jnp.bfloat16),
            jax.ShapeDtypeStruct((batch_rows, classes), jnp.float32),
        ),
        in_specs=[smem] + [vmem] * 5,
        out_specs=(hbm, hbm),
        scratch_shapes=[
            pltpu.VMEM((blocks * batch_total * LINES, LANES), jnp.float32),
            pltpu.VMEM((pl.cdiv(classes, LANES) * LANES, 4 * batch_total), jnp.bfloat16),
            pltpu.VMEM((4 * batch_total, center_rows), jnp.bfloat16),
            pltpu.VMEM((classes, center_rows), jnp.bfloat16),
            pltpu.VMEM((batch_rows, classes), jnp.float32),
            pltpu.SemaphoreType.DMA((1 + slab_count * pl.cdiv(classes, chunk),)),
        ],
        compiler_params=params,
        name="update",
    )(wide_pos[None], both, eig_scale[None, :], kern, vecs, kept)
    return (new_turned.T, residual)


def solution(mesh):
    return jax.shard_map(
        shards,
        mesh=mesh,
        in_specs=(
            P("wide", None),
            P("wide", None),
            P("wide"),
            P(("sec", "wide"), None),
            P(("sec", "wide"), None),
            P("wide"),
            P("wide", None),
            P(),
        ),
        out_specs=(P(("sec", "wide"), None), P("wide", None)),
        check_vma=False,
    )
```
